32 devices in a mesh: row: 8 (over z, y), col: 4 (over x, core).
Axes of the slice: x: 2, y: 2, z: 4, core: 2. Of those that a mesh axis runs over, the one named last changes fastest.
Arguments:
- inputs: bfloat16 [768, 8192], P('row', 'col'), may hold values from -16 to 16
- norm_gain: float32 [8192], P('col'), may hold values from 0.25 to 4
- w_gate: bfloat16 [8192, 28672], P('col', 'row'), may hold values from -0.09375 to 0.09375
- w_up: bfloat16 [8192, 28672], P('col', 'row'), may hold values from -0.09375 to 0.09375
- w_down: bfloat16 [28672, 8192], P('row', 'col'), may hold values from -0.050111483 to 0.050111483
- mask_gate: int32 [128, 448], P('col', 'row'), may hold values 0 or 1
- mask_up: int32 [128, 448], P('col', 'row'), may hold values 0 or 1
- mask_down: int32 [448, 128], P('row', 'col'), may hold values 0 or 1
- grad_out: bfloat16 [768, 8192], P('row', 'col'), may hold values from -5 to 5
Outputs:
- output: bfloat16 [768, 8192], P('row', 'col')
- grad_inputs: bfloat16 [768, 8192], P('row', 'col')
- grad_gain: float32 [8192], P('col')
- grad_w_gate: bfloat16 [8192, 28672], P('col', 'row')
- grad_w_up: bfloat16 [8192, 28672], P('col', 'row')
- grad_w_down: bfloat16 [28672, 8192], P('row', 'col')
The draws below stay inside these ranges and needn't reach their ends.
All inputs are finite; a program needn't handle non-finite values. No bound on the sum of `mask_gate` or of `mask_up` or of `mask_down` on one device may be relied on, other than what follows from the above.
Results may differ from the reference program's by a relative error of at most 0.02.
Values may be sent and summed in bfloat16 or wider, within the bound.
No kernel may reach another device: no remote copies, remote signals or barrier semaphores. Data moves between devices by JAX's collectives and lax.ppermute only.
A program may use at most 256 MiB of HBM per device.

```python
import jax
import jax.numpy as jnp
from jax import lax

D = 8192
FF = 28672
BLOCK = 64
TOKENS = 768
N_ROW = 8
N_COL = 4


def feature_ramp(low_end, high_end):
    position = jnp.arange(D, dtype=jnp.float32) / max(D - 1, 1)
    return low_end * jnp.exp(position * jnp.log(high_end / low_end))


def unit_noise(noise_key, shape):
    return jax.random.truncated_normal(noise_key, -4.0, 4.0, shape, jnp.float32)


def feature_signs(key):
    picked = jax.random.bernoulli(jax.random.fold_in(key, 21), 0.5, (D,))
    return jnp.where(picked, 1.0, -1.0).astype(jnp.float32)


def shared_gate_noise(key):
    return unit_noise(jax.random.fold_in(key, 11), (D, FF))


def draw_inputs(key, part):
    first_key, second_key = jax.random.split(key)
    ramp = feature_ramp(1.0, 3.0) * jax.random.uniform(second_key, (D,), jnp.float32, 0.8, 1.25)
    values = jax.random.truncated_normal(first_key, -4.0, 4.0, (TOKENS, D), jnp.float32)
    return (values * ramp).astype(jnp.bfloat16)


def draw_norm_gain(key, part):
    ramp = feature_ramp(0.5, 2.0) * jax.random.uniform(key, (D,), jnp.float32, 0.8, 1.25)
    return ramp.astype(jnp.float32)


def draw_w_gate(key, part):
    spread = float(D // 2) ** (-0.5)
    return (shared_gate_noise(key) * spread).astype(jnp.bfloat16)


def draw_w_up(key, part):
    spread = float(D // 2) ** (-0.5)
    linked = 0.9
    own_noise = unit_noise(jax.random.fold_in(key, 12), (D, FF))
    mixed = linked * shared_gate_noise(key) + (1.0 - linked * linked) ** 0.5 * own_noise
    return (mixed * spread).astype(jnp.bfloat16)


def draw_w_down(key, part):
    spread = float(FF // 2) ** (-0.5)
    offset = 4.0 / FF
    noise = unit_noise(jax.random.fold_in(key, 13), (FF, D))
    return (noise * spread + offset * feature_signs(key)[None, :]).astype(jnp.bfloat16)


def draw_grad_out(key, part):
    amplitude = jax.random.uniform(jax.random.fold_in(key, 31), (TOKENS, 1), jnp.float32, 0.3, 0.6)
    noise = unit_noise(jax.random.fold_in(key, 14), (TOKENS, D))
    return (noise + amplitude * feature_signs(key)[None, :]).astype(jnp.bfloat16)


def touch_ends(entries, rng, low, largest):
    place = [jax.random.randint(jax.random.fold_in(rng, axis), (), 0, length) for axis, length in enumerate(entries.shape)]
    longest = entries.shape.index(max(entries.shape))
    beside = place[:longest] + [(place[longest] + 1) % entries.shape[longest]] + place[longest + 1:]
    return entries.at[tuple(place)].set(low).at[tuple(beside)].set(largest)


def setup_inputs(seed: int = 0) -> dict:
    keys = jax.random.split(jax.random.key(seed), 10)
    inputs = draw_inputs(jax.random.fold_in(keys[9], 71), 0)
    norm_gain = draw_norm_gain(jax.random.fold_in(keys[9], 71), 0)
    w_gate = draw_w_gate(jax.random.fold_in(keys[9], 71), 0)
    w_up = draw_w_up(jax.random.fold_in(keys[9], 71), 0)
    w_down = draw_w_down(jax.random.fold_in(keys[9], 71), 0)
    mask_gate = touch_ends((jax.random.randint(keys[5], (D // BLOCK, FF // BLOCK), 0, 2) < 1).astype(jnp.int32), jax.random.fold_in(keys[5], 1), 0, 1)
    mask_up = touch_ends((jax.random.randint(keys[6], (D // BLOCK, FF // BLOCK), 0, 2) < 1).astype(jnp.int32), jax.random.fold_in(keys[6], 1), 0, 1)
    mask_down = touch_ends((jax.random.randint(keys[7], (FF // BLOCK, D // BLOCK), 0, 2) < 1).astype(jnp.int32), jax.random.fold_in(keys[7], 1), 0, 1)
    grad_out = draw_grad_out(jax.random.fold_in(keys[9], 71), 0)
    return {"inputs": inputs, "norm_gain": norm_gain, "w_gate": w_gate, "w_up": w_up, "w_down": w_down, "mask_gate": mask_gate, "mask_up": mask_up, "mask_down": mask_down, "grad_out": grad_out}


epsilon = 1e-05

def expand_mask(weight, block_mask):
    mask_rows, mask_cols = block_mask.shape
    blocked = weight.reshape(mask_rows, BLOCK, mask_cols, BLOCK) * block_mask.astype(jnp.bfloat16)[:, None, :, None]
    return blocked.reshape(weight.shape)

def contract_rows(left, right):
    return lax.dot_general(left, right, (((0,), (0,)), ((), ())), preferred_element_type=jnp.float32)

def piecewise(pairs, pieces, left_axis, right_axis):
    width = pairs[0][0].shape[left_axis] // pieces
    total = None
    for index in range(pieces):
        term = None
        for left, right in pairs:
            left_piece = lax.slice_in_dim(left, index * width, (index + 1) * width, axis=left_axis)
            right_piece = lax.slice_in_dim(right, index * width, (index + 1) * width, axis=right_axis)
            product = lax.dot_general(left_piece, right_piece, (((left_axis,), (right_axis,)), ((), ())), preferred_element_type=jnp.float32)
            term = product if term is None else term + product
        rounded = lax.optimization_barrier(term.astype(jnp.bfloat16)).astype(jnp.float32)
        total = rounded if total is None else total + rounded
    return total

def reference(inputs, norm_gain, w_gate, w_up, w_down, mask_gate, mask_up, mask_down, grad_out):
    gate_eff = expand_mask(w_gate, mask_gate)
    up_eff = expand_mask(w_up, mask_up)
    down_eff = expand_mask(w_down, mask_down)
    inputs_wide = inputs.astype(jnp.float32)
    inv_rms = lax.rsqrt(lax.optimization_barrier(jnp.mean(inputs_wide * inputs_wide, axis=1, keepdims=True)) + epsilon)
    normed = inputs_wide * inv_rms
    hidden_in = (normed * norm_gain).astype(jnp.bfloat16)
    gate_value = piecewise([(hidden_in, gate_eff)], N_COL, 1, 0)
    up_value = piecewise([(hidden_in, up_eff)], N_COL, 1, 0)
    sigmoid_gate = jax.nn.sigmoid(gate_value)
    silu_gate = gate_value * sigmoid_gate
    hidden = (silu_gate * up_value).astype(jnp.bfloat16)
    output = (inputs_wide + piecewise([(hidden, down_eff)], N_ROW, 1, 0)).astype(jnp.bfloat16)
    d_hidden = piecewise([(grad_out, down_eff)], N_COL, 1, 1)
    grad_w_down = expand_mask(contract_rows(hidden, grad_out).astype(jnp.bfloat16), mask_down)
    d_up = (d_hidden * silu_gate).astype(jnp.bfloat16)
    d_gate = (d_hidden * up_value * sigmoid_gate * (1.0 + gate_value * (1.0 - sigmoid_gate))).astype(jnp.bfloat16)
    grad_w_gate = expand_mask(contract_rows(hidden_in, d_gate).astype(jnp.bfloat16), mask_gate)
    grad_w_up = expand_mask(contract_rows(hidden_in, d_up).astype(jnp.bfloat16), mask_up)
    d_norm_in = piecewise([(d_gate, gate_eff), (d_up, up_eff)], N_ROW, 1, 1)
    grad_gain = lax.optimization_barrier(jnp.sum(d_norm_in * normed, axis=0))
    d_normed = d_norm_in * norm_gain
    row_inner = lax.optimization_barrier(jnp.sum(d_normed * normed, axis=1, keepdims=True)) / D
    grad_inputs = (grad_out.astype(jnp.float32) + inv_rms * (d_normed - normed * row_inner)).astype(jnp.bfloat16)
    return (output, grad_inputs, grad_gain, grad_w_gate, grad_w_up, grad_w_down)
```

```python
import functools

import jax
import jax.numpy as jnp
from jax import lax
from jax.experimental import pallas as pl
from jax.experimental.pallas import tpu as pltpu
from jax.sharding import PartitionSpec as P

BLOCK = 64
CORES = 2
epsilon = 1e-05
bf16 = jnp.bfloat16
f32 = jnp.float32


def tile_of(size, limit):
    best = 128
    for tile in range(128, limit + 1, 128):
        if size % tile == 0:
            best = tile
    return best


def lanes(block_mask):
    rows, cols = block_mask.shape
    wide = jnp.broadcast_to(block_mask.astype(f32)[:, :, None], (rows, cols, BLOCK))
    return lax.optimization_barrier(wide.reshape(rows, cols * BLOCK))


def dot(left, right, left_axis, right_axis):
    return lax.dot_general(
        left, right, (((left_axis,), (right_axis,)), ((), ())), preferred_element_type=f32
    )


def keep_rows(mask_ref, row, cols):
    keep = jnp.broadcast_to(mask_ref[pl.ds(row, 1), :], (16, cols))
    return keep.astype(bf16)[None]


def block_rows(value, keep):
    cols = value.shape[1]
    return (value.reshape(BLOCK // 16, 16, cols) * keep).reshape(BLOCK, cols)


def whole(array):
    return pl.BlockSpec(array.shape, lambda *_: (0,) * array.ndim)


def call(body, grid, scalars, operands, in_specs, out_specs, out_shape, scratch,
         flops, moved, aliases=None):
    return pl.pallas_call(
        body,
        grid_spec=pltpu.PrefetchScalarGridSpec(
            num_scalar_prefetch=1,
            grid=grid,
            in_specs=in_specs,
            out_specs=out_specs,
            scratch_shapes=scratch,
        ),
        out_shape=out_shape,
        input_output_aliases=aliases or {},
        compiler_params=pltpu.CompilerParams(vmem_limit_bytes=60 << 20),
        cost_estimate=pl.CostEstimate(
            flops=int(flops), bytes_accessed=int(moved), transcendentals=0),
    )(scalars, *operands)


class Plan:
    def __init__(self, width):
        self.half = width // CORES
        self.tile = tile_of(self.half, 256)
        self.count = self.half // self.tile
        first = (self.count + 1) // 2
        self.chunks = [(0, first)]
        if self.count > first:
            self.chunks.append((first, self.count - first))


def mask_columns(plan, chunk, scalars, w_gate, w_up, gate_lanes, up_lanes):
    first, steps = chunk
    depth, tile = w_gate.shape[0], plan.tile

    def body(_, g_ref, u_ref, gm_ref, um_ref, out_ref):
        for w_ref, k_ref, lane in ((g_ref, gm_ref, 0), (u_ref, um_ref, tile)):
            for index in range(depth // BLOCK):
                span = pl.ds(index * BLOCK, BLOCK)
                out_ref[span, lane:lane + tile] = block_rows(
                    w_ref[span, :], keep_rows(k_ref, index, tile))

    column = lambda h, j, s: (0, h * plan.count + first + j)
    weight = pl.BlockSpec((depth, tile), column)
    mask = pl.BlockSpec((depth // BLOCK, tile), column)
    return call(
        body, (CORES, steps), scalars, (w_gate, w_up, gate_lanes, up_lanes),
        [weight, weight, mask, mask],
        pl.BlockSpec((depth, 2 * tile), lambda h, j, s: (0, h * steps + j)),
        jax.ShapeDtypeStruct((depth, CORES * steps * 2 * tile), bf16), [],
        0, 8 * CORES * depth * steps * tile)


def mask_rows(plan, chunk, scalars, w_down, down_lanes):
    first, steps = chunk
    depth, tile = w_down.shape[1], plan.tile

    def body(_, w_ref, k_ref, out_ref):
        start = pl.program_id(0) * plan.count + first + pl.program_id(1)
        for index in range(tile // BLOCK):
            span = pl.ds(index * BLOCK, BLOCK)
            keep = keep_rows(k_ref, start * (tile // BLOCK) + index, depth)
            out_ref[span, :] = block_rows(w_ref[span, :], keep)

    return call(
        body, (CORES, steps), scalars, (w_down, down_lanes),
        [pl.BlockSpec((tile, depth), lambda h, j, s: (h * plan.count + first + j, 0)),
         whole(down_lanes)],
        pl.BlockSpec((tile, depth), lambda h, j, s: (h * steps + j, 0)),
        jax.ShapeDtypeStruct((CORES * steps * tile, depth), bf16), [],
        0, 4 * CORES * depth * steps * tile)


def project(side, halves, tokens, weight, added=None):
    rows, depth = tokens.shape
    width = weight.shape[1] // CORES
    tile = tile_of(width, 512)
    steps = width // tile

    def body(_, x_ref, w_ref, *rest):
        value = dot(x_ref[...], w_ref[...], 1, 0)
        if added is not None:
            value += rest[0][...].astype(f32)
        rest[-1][...] = value.astype(bf16)

    out = pl.BlockSpec((rows, tile), lambda i, h: (0, i))
    extra = () if added is None else (added,)
    return call(
        body, (steps,), halves, (tokens, weight, *extra),
        [whole(tokens), pl.BlockSpec((depth, tile), lambda i, h: (0, h[side] * steps + i))]
        + [out] * len(extra),
        out, jax.ShapeDtypeStruct((rows, width), bf16), [],
        2 * rows * depth * width, 2 * depth * width + 2 * rows * depth + 2 * rows * width)


def back_project(side, halves, tokens, weight, added=None):
    rows, depth = tokens.shape
    width = weight.shape[0] // CORES
    tile = tile_of(width, 256)
    steps = width // tile

    def body(_, g_ref, w_ref, *rest):
        value = dot(g_ref[...], w_ref[...], 1, 1)
        if added is not None:
            value += rest[0][...].astype(f32)
        rest[-1][...] = value.astype(bf16)

    out = pl.BlockSpec((rows, tile), lambda i, h: (0, i))
    extra = () if added is None else (added,)
    return call(
        body, (steps,), halves, (tokens, weight, *extra),
        [whole(tokens), pl.BlockSpec((tile, depth), lambda i, h: (h[side] * steps + i, 0))]
        + [out] * len(extra),
        out, jax.ShapeDtypeStruct((rows, width), bf16), [],
        2 * rows * depth * width, 2 * depth * width + 2 * rows * depth + 2 * rows * width)


def activate(plan, scalars, scale, pieces, grad_pieces, start, stop):
    tile = plan.tile
    width = pieces[0][1][0].shape[1] // 2
    with_grad = grad_pieces is not None
    cuts = {start, stop}
    listed = list(pieces) + (list(grad_pieces) if with_grad else [])
    for first, arrays in listed:
        cuts |= {first, first + arrays[0].shape[0]}
    cuts = sorted(cut for cut in cuts if start <= cut <= stop)
    operands, in_specs = [scale], [whole(scale)]
    for first, arrays in pieces:
        operands += arrays
        in_specs += [pl.BlockSpec((a.shape[0], 2 * tile), lambda j, s: (0, j)) for a in arrays]
    for first, arrays in grad_pieces or ():
        operands += arrays
        in_specs += [pl.BlockSpec((a.shape[0], tile), lambda j, s: (0, j)) for a in arrays]
    rows = stop - start
    wide = 2 * tile if with_grad else tile

    def summed(refs, groups, low, high, lane):
        position = 0
        for first, arrays in groups:
            if first <= low and high <= first + arrays[0].shape[0]:
                total = None
                for ref in refs[position:position + len(arrays)]:
                    term = ref[low - first:high - first, lane:lane + tile].astype(f32)
                    total = term if total is None else total + term
                return total
            position += len(arrays)

    def body(_, s_ref, *refs):
        out_ref = refs[-1]
        count = sum(len(arrays) for _, arrays in pieces)
        for low, high in zip(cuts[:-1], cuts[1:]):
            span = slice(low - start, high - start)
            factor = s_ref[low:high, :]
            gate = summed(refs, pieces, low, high, 0) * factor
            up = summed(refs, pieces, low, high, tile) * factor
            sigma = jax.nn.sigmoid(gate)
            if with_grad:
                grad = summed(refs[count:], grad_pieces, low, high, 0)
                d_gate = grad * up * sigma * (1.0 + gate * (1.0 - sigma))
                out_ref[span, :tile] = d_gate.astype(bf16)
                out_ref[span, tile:] = (grad * (gate * sigma)).astype(bf16)
            else:
                out_ref[span, :] = (gate * sigma * up).astype(bf16)

    return call(
        body, (width // tile,), scalars, operands, in_specs,
        pl.BlockSpec((rows, wide), lambda j, s: (0, j)),
        jax.ShapeDtypeStruct((rows, width // tile * wide), bf16), [],
        0, 2 * sum(a.size for a in operands) + 2 * rows * width)


def down_product(halves, hidden, weights):
    rows, depth = hidden[0][0].shape[0], weights[0].shape[1]
    tile = tile_of(depth, 256)
    operands, in_specs = [], []
    for pair, weight in zip(hidden, weights):
        width = weight.shape[0] // CORES
        for side, value in enumerate(pair):
            operands += [value, weight]
            in_specs += [whole(value), pl.BlockSpec(
                (width, tile), lambda i, h, side=side: (h[side], i))]

    def body(_, *refs):
        value = None
        for h_ref, w_ref in zip(refs[:-1:2], refs[1:-1:2]):
            term = dot(h_ref[...], w_ref[...], 1, 0)
            value = term if value is None else value + term
        refs[-1][...] = value.astype(bf16)

    total = sum(weight.size for weight in weights)
    return call(
        body, (depth // tile,), halves, operands, in_specs,
        pl.BlockSpec((rows, tile), lambda i, h: (0, i)),
        jax.ShapeDtypeStruct((rows, depth), bf16), [],
        2 * rows * total, 2 * total + 2 * rows * (total // depth + depth))


def input_cotangent(halves, pair, weight, start, added, dtype):
    rows = pair[0].shape[0]
    depth, width = weight.shape[0], weight.shape[1] // CORES
    tile = tile_of(depth, 256)
    side = [pl.BlockSpec((tile, width), lambda i, h: (i, h[0])),
            pl.BlockSpec((tile, width), lambda i, h: (i, h[1]))]
    extra = () if added is None else (added,)

    def body(_, m_ref, o_ref, wm_ref, wo_ref, *rest):
        value = dot(m_ref[...], wm_ref[...], 1, 1) + dot(o_ref[...], wo_ref[...], 1, 1)
        if added is not None:
            value += rest[0][start:start + rows, :]
        rest[-1][...] = value.astype(dtype)

    return call(
        body, (depth // tile,), halves, (*pair, weight, weight, *extra),
        [whole(pair[0]), whole(pair[1]), *side]
        + [pl.BlockSpec((a.shape[0], tile), lambda i, h: (0, i)) for a in extra],
        pl.BlockSpec((rows, tile), lambda i, h: (0, i)),
        jax.ShapeDtypeStruct((rows, depth), dtype), [],
        2 * rows * weight.size, 2 * weight.size + 4 * rows * width + 4 * rows * depth)


def turn(scalars, scale, pieces):
    rows, depth = scale.shape[0], pieces[0].shape[1]
    tile = tile_of(depth, 256)

    def body(_, s_ref, *refs):
        out_ref, scratch = refs[-2:]
        first = 0
        for ref in refs[:-2]:
            span = slice(first, first + ref.shape[0])
            scratch[span, :] = (ref[...].astype(f32) * s_ref[span, :]).astype(bf16)
            first += ref.shape[0]
        out_ref[...] = scratch[...].T

    return call(
        body, (depth // tile,), scalars, (scale, *pieces),
        [whole(scale)] + [pl.BlockSpec((p.shape[0], tile), lambda i, s: (0, i)) for p in pieces],
        pl.BlockSpec((tile, rows), lambda i, s: (i, 0)),
        jax.ShapeDtypeStruct((depth, rows), bf16), [pltpu.VMEM((rows, tile), bf16)],
        0, 4 * rows * depth)


def gate_up_grads(plan, chunk, halves, turned, mine, other, gate_lanes, up_lanes, earlier,
                  single=None):
    first, steps = chunk
    skipped = 0
    if single is not None:
        first, steps, skipped = first + single, 1, single
    depth, rows = turned.shape
    tile = plan.tile
    n_mine = len(mine)

    def body(_, x_ref, *refs):
        sides = refs[:n_mine], refs[n_mine:2 * n_mine]
        masks = refs[2 * n_mine:2 * n_mine + 2]
        outs, scratch = refs[-3:-1], refs[-1]

        def collect(pieces):
            row = 0
            for ref in pieces:
                scratch[row:row + ref.shape[0], :] = ref[...]
                row += ref.shape[0]

        pl.when(pl.program_id(0) == 0)(lambda: collect(sides[0]))
        pl.when(pl.program_id(0) == 1)(lambda: collect(sides[1]))
        for index in range(2):
            right = scratch[:, index * tile:(index + 1) * tile]
            value = dot(x_ref[...], right, 1, 0).astype(bf16)
            for block in range(depth // BLOCK):
                span = slice(block * BLOCK, (block + 1) * BLOCK)
                outs[index][span, :] = block_rows(
                    value[span, :], keep_rows(masks[index], block, tile))

    column = lambda p, j, h: (0, h[p] * plan.count + first + j)
    in_specs = [whole(turned)]
    in_specs += [pl.BlockSpec((a.shape[0], 2 * tile), lambda p, j, h: (
        0, skipped + jnp.where(p == 0, j, steps - 1))) for a in mine]
    in_specs += [pl.BlockSpec((a.shape[0], 2 * tile), lambda p, j, h: (
        0, skipped + jnp.where(p == 0, 0, j))) for a in other]
    in_specs += [pl.BlockSpec((depth // BLOCK, tile), column)] * 2
    out = pl.BlockSpec((depth, tile), column)
    shape = jax.ShapeDtypeStruct((depth, plan.half * CORES), bf16)
    operands = [turned, *mine, *other, gate_lanes, up_lanes]
    aliases = None
    if earlier is not None:
        aliases = {len(operands) + 1: 0, len(operands) + 2: 1}
        operands += earlier
        in_specs += [pl.BlockSpec(memory_space=pl.ANY)] * 2
    return call(
        body, (CORES, steps), halves, operands, in_specs, [out, out], [shape, shape],
        [pltpu.VMEM((rows, 2 * tile), bf16)],
        8 * rows * depth * steps * tile,
        2 * rows * depth + 8 * rows * steps * tile + 8 * depth * steps * tile, aliases)


def down_grads(plan, halves, hidden, grads, down_lanes):
    rows, depth = hidden[0][0].shape[0], grads[0].shape[1]
    tile = tile_of(depth, 256)
    operands, places = [], []
    for pair, (first, steps) in zip(hidden, plan.chunks):
        for side, value in enumerate(pair):
            operands.append(value)
            places.append((side, first * plan.tile))
    count = len(operands)
    width = plan.half * CORES

    def body(half_ref, *refs):
        turned, right, out_ref = refs[-2], refs[-1], refs[-3]

        @pl.when(pl.program_id(0) == 0)
        def _():
            for ref, (side, first) in zip(refs[:count], places):
                start = pl.multiple_of(half_ref[side] * plan.half + first, 128)
                for lane in range(0, ref.shape[1], plan.tile):
                    turned[pl.ds(start + lane, plan.tile), :] = ref[:, lane:lane + plan.tile].T

        row = 0
        for ref in refs[count:count + len(grads)]:
            right[row:row + ref.shape[0], :] = ref[...]
            row += ref.shape[0]
        k_ref = refs[count + len(grads)]
        piece = plan.tile
        for part in range(width // piece):
            value = dot(turned[part * piece:(part + 1) * piece, :], right[...], 1, 0).astype(bf16)
            for block in range(piece // BLOCK):
                low = part * piece + block * BLOCK
                out_ref[low:low + BLOCK, :] = block_rows(
                    value[block * BLOCK:(block + 1) * BLOCK, :],
                    keep_rows(k_ref, low // BLOCK, tile))

    column = lambda i, h: (0, i)
    return call(
        body, (depth // tile,), halves, (*operands, *grads, down_lanes),
        [whole(value) for value in operands]
        + [pl.BlockSpec((g.shape[0], tile), column) for g in grads]
        + [pl.BlockSpec((down_lanes.shape[0], tile), column)],
        pl.BlockSpec((width, tile), column),
        jax.ShapeDtypeStruct((width, depth), bf16),
        [pltpu.VMEM((width, rows), bf16), pltpu.VMEM((rows, tile), bf16)],
        2 * rows * depth * width, 2 * depth * width + 2 * rows * width + 2 * rows * depth)


def after(value, *others):
    return lax.optimization_barrier((value, *others))[0]


def shards(n_row, n_col, inputs, norm_gain, w_gate, w_up, w_down,
           mask_gate, mask_up, mask_down, grad_out):
    n_chip = n_col // CORES
    local, width = inputs.shape
    features = width * n_col
    plan = Plan(w_gate.shape[1])
    chunks = plan.chunks
    cycle = list(range(0, n_row, 2)) + list(range(n_row - 1, 0, -2))
    ahead = [(cycle[i], cycle[(i + 1) % n_row]) for i in range(n_row)]
    behind = [(b, a) for a, b in ahead]
    swap = [(i, i ^ 1) for i in range(n_col)]
    n_ahead, n_behind = n_row // 2, (n_row - 1) // 2

    def to_partner(value):
        return lax.ppermute(value, "col", swap)

    def from_chips(value):
        return [
            lax.ppermute(value, "col", [(i, (i + CORES * k) % n_col) for i in range(n_col)])
            for k in range(1, n_chip)
        ]

    def total_over_chips(value):
        total = value
        for other in from_chips(value):
            total = total + other
        return total

    offsets = [0]
    for k in range(1, n_ahead + 1):
        offsets.append(-k)
        if k <= n_behind:
            offsets.append(k)
    near, far = offsets[:3], offsets[3:]
    rows_near = local * len(near)
    rows_all = local * len(offsets)

    core = lax.rem(lax.axis_index("col"), CORES).astype(jnp.int32)
    halves = jnp.stack([core, 1 - core])

    inputs_wide = inputs.astype(f32)
    scaled = (inputs_wide * norm_gain).astype(bf16)
    gate_lanes, up_lanes, down_lanes = lanes(mask_gate), lanes(mask_up), lanes(mask_down)

    def ring_step(found, k, *ready):
        found[-k] = lax.ppermute(after(found[1 - k], *ready), "row", ahead)
        if k <= n_behind:
            found[k] = lax.ppermute(after(found[k - 1], *ready), "row", behind)

    def rows_of(found, group):
        return jnp.concatenate([found[offset] for offset in group], axis=0)

    shard = {0: scaled}
    ring_step(shard, 1)
    gu = [mask_columns(plan, chunks[0], halves, w_gate, w_up, gate_lanes, up_lanes)]
    ring_step(shard, 2, gu[0])
    gu.append(mask_columns(plan, chunks[1], after(halves, gu[0]),
                           w_gate, w_up, gate_lanes, up_lanes))
    ring_step(shard, 3, gu[1])
    tokens_near = rows_of(shard, near)
    sent_near = project(1, after(halves, gu[1]), tokens_near, gu[0])
    for k in range(4, n_ahead + 1):
        ring_step(shard, k, sent_near)
    squares = jnp.sum(jnp.square(tokens_near.astype(f32) / norm_gain), axis=1)
    own_near = project(0, halves, tokens_near, gu[0], to_partner(sent_near))
    others_near = from_chips(own_near)

    tokens_far = rows_of(shard, far)
    squares_far = jnp.sum(jnp.square(tokens_far.astype(f32) / norm_gain), axis=1)
    squares = jnp.concatenate([squares, squares_far])
    sent_far = project(1, halves, after(tokens_far, own_near), gu[0])
    grad_shard = {0: after(grad_out, tokens_far)}
    ring_step(grad_shard, 1)
    dn = [mask_rows(plan, chunks[0], after(halves, sent_far), w_down, down_lanes)]
    own_far = project(0, after(halves, dn[0]), tokens_far, gu[0], to_partner(sent_far))
    others_far = from_chips(after(own_far, *others_near))
    ring_step(grad_shard, 2, own_far)
    dn.append(mask_rows(plan, chunks[1], after(halves, own_far), w_down, down_lanes))
    ring_step(grad_shard, 3, dn[1])
    squares = squares + to_partner(after(squares, own_far))
    squares = total_over_chips(squares)
    scale = lax.rsqrt(squares / features + epsilon)[:, None]
    tokens_all = jnp.concatenate([tokens_near, tokens_far], axis=0)
    sent_next = project(1, after(halves, dn[1]), tokens_all, gu[1])
    for k in range(4, n_ahead + 1):
        ring_step(grad_shard, k, sent_next)
    own_next = project(0, halves, tokens_all, gu[1], to_partner(sent_next))
    grads_near, grads_far = rows_of(grad_shard, near), rows_of(grad_shard, far)
    grads_all = jnp.concatenate([grads_near, grads_far], axis=0)
    sent_grad = back_project(1, after(halves, own_next), grads_all, dn[0])
    turned = turn(after(halves, sent_grad), scale, [tokens_near, tokens_far])
    own_grad = back_project(0, after(halves, turned), grads_all, dn[0],
                            to_partner(sent_grad))
    others_grad = from_chips(after(own_grad, *others_far))
    sent_gf = back_project(1, after(halves, own_grad), grads_far, dn[1])
    sent_gn = back_project(1, after(halves, sent_gf), grads_near, dn[1])
    own_gf = back_project(0, after(halves, sent_gn), grads_far, dn[1],
                          to_partner(sent_gf))
    own_gn = back_project(0, after(halves, own_gf), grads_near, dn[1],
                          to_partner(sent_gn))

    pieces0 = [(0, [own_near, *others_near]), (rows_near, [own_far, *others_far])]
    hidden0 = activate(plan, after(halves, own_gn), scale, pieces0, None, 0, rows_all)
    hidden0 = (hidden0, to_partner(hidden0))
    others_next = from_chips(after(own_next, *others_grad))
    cot0 = activate(plan, after(halves, hidden0[0]), scale, pieces0, [(0, [own_grad, *others_grad])],
                    0, rows_all)
    cot0 = (cot0, to_partner(cot0))
    partial = input_cotangent(halves, cot0, gu[0], 0, None, f32)
    grad_gu = gate_up_grads(plan, chunks[0], after(halves, partial), turned,
                            cot0[:1], cot0[1:], gate_lanes, up_lanes, None)

    pieces1 = [(0, [own_next, *others_next])]
    hidden1 = activate(plan, after(halves, grad_gu[0]), scale, pieces1, None, 0, rows_all)
    hidden1 = (hidden1, to_partner(hidden1))
    others_gf = from_chips(after(own_gf, *others_next))
    mixed = down_product(halves, (hidden0, hidden1), dn)

    def scatter(parts):
        back = parts(-n_ahead)
        front = parts(n_behind)
        for k in range(1, n_ahead + 1):
            back = lax.ppermute(back, "row", behind)
            if k < n_ahead:
                back = (back.astype(f32) + parts(k - n_ahead).astype(f32)).astype(bf16)
            if k <= n_behind:
                front = lax.ppermute(front, "row", ahead)
                if k < n_behind:
                    front = (front.astype(f32) + parts(n_behind - k).astype(f32)).astype(bf16)
        return back.astype(f32) + front.astype(f32) + parts(0).astype(f32)

    def part_of(value, group):
        return {offset: lax.slice_in_dim(value, i * local, (i + 1) * local, axis=0)
                for i, offset in enumerate(group)}

    parts = part_of(mixed, offsets)
    output = (inputs_wide + scatter(lambda offset: parts[offset])).astype(bf16)
    grad_w_down = down_grads(plan, after(halves, mixed), (hidden0, hidden1),
                             (grads_near, grads_far), down_lanes)

    others_gn = from_chips(after(own_gn, *others_gf))
    cot_far = activate(plan, after(halves, grad_w_down), scale, pieces1,
                       [(rows_near, [own_gf, *others_gf])], rows_near, rows_all)
    cot_far = (cot_far, to_partner(cot_far))
    norm_far = input_cotangent(halves, cot_far, gu[1], rows_near, partial, bf16)
    cot_near = activate(plan, after(halves, norm_far), scale, pieces1,
                        [(0, [own_gn, *others_gn])], 0, rows_near)
    cot_near = (cot_near, to_partner(cot_near))
    norm_near = input_cotangent(halves, cot_near, gu[1], 0, partial, bf16)
    norms = {**part_of(norm_far, far), **part_of(norm_near, near)}
    d_norm_in = scatter(lambda offset: norms[offset])
    ready = norm_near
    for index in range(chunks[1][1]):
        grad_gu = gate_up_grads(
            plan, chunks[1], after(halves, ready), turned,
            (cot_near[0], cot_far[0]), (cot_near[1], cot_far[1]), gate_lanes, up_lanes, grad_gu,
            index)
        ready = grad_gu[0]
    grad_w_gate, grad_w_up = grad_gu

    inv_local = scale[:local]
    normed = inputs_wide * inv_local
    d_normed = d_norm_in * norm_gain
    inner = jnp.sum(d_normed * normed, axis=1)
    inner = total_over_chips(inner + to_partner(inner)) / features
    gain_part = jnp.sum(d_norm_in * normed, axis=0)
    step = 1
    while step < n_row:
        gain_part = gain_part + lax.ppermute(
            gain_part, "row", [(i, i ^ step) for i in range(n_row)])
        step *= 2
    grad_inputs = (
        grad_out.astype(f32) + inv_local * (d_normed - normed * inner[:, None])
    ).astype(bf16)
    return (output, grad_inputs, gain_part, grad_w_gate, grad_w_up, grad_w_down)


def solution(mesh):
    in_specs = (
        P("row", "col"),
        P("col"),
        P("col", "row"),
        P("col", "row"),
        P("row", "col"),
        P("col", "row"),
        P("col", "row"),
        P("row", "col"),
        P("row", "col"),
    )
    out_specs = (
        P("row", "col"),
        P("row", "col"),
        P("col"),
        P("col", "row"),
        P("col", "row"),
        P("row", "col"),
    )
    body = functools.partial(shards, mesh.shape["row"], mesh.shape["col"])

    return jax.shard_map(
        body, mesh=mesh, in_specs=in_specs, out_specs=out_specs, check_vma=False)
```

```python
import functools

import jax
import jax.numpy as jnp
from jax import lax
from jax.experimental import pallas as pl
from jax.experimental.pallas import tpu as pltpu
from jax.sharding import PartitionSpec as P

BLOCK = 64
CORES = 2
epsilon = 1e-05
bf16 = jnp.bfloat16
f32 = jnp.float32


def tile_of(size, limit):
    best = 128
    for tile in range(128, limit + 1, 128):
        if size % tile == 0:
            best = tile
    return best


def lanes(block_mask):
    rows, cols = block_mask.shape
    wide = jnp.broadcast_to(block_mask.astype(f32)[:, :, None], (rows, cols, BLOCK))
    return lax.optimization_barrier(wide.reshape(rows, cols * BLOCK))


def dot(left, right, left_axis, right_axis):
    return lax.dot_general(
        left, right, (((left_axis,), (right_axis,)), ((), ())), preferred_element_type=f32
    )


def keep_rows(mask_ref, row, cols):
    keep = jnp.broadcast_to(mask_ref[pl.ds(row, 1), :], (16, cols))
    return keep.astype(bf16)[None]


def block_rows(value, keep):
    cols = value.shape[1]
    return (value.reshape(BLOCK // 16, 16, cols) * keep).reshape(BLOCK, cols)


def whole(array):
    return pl.BlockSpec(array.shape, lambda *_: (0,) * array.ndim)


def call(body, grid, scalars, operands, in_specs, out_specs, out_shape, scratch,
         flops, moved, aliases=None):
    return pl.pallas_call(
        body,
        grid_spec=pltpu.PrefetchScalarGridSpec(
            num_scalar_prefetch=1,
            grid=grid,
            in_specs=in_specs,
            out_specs=out_specs,
            scratch_shapes=scratch,
        ),
        out_shape=out_shape,
        input_output_aliases=aliases or {},
        compiler_params=pltpu.CompilerParams(vmem_limit_bytes=60 << 20),
        cost_estimate=pl.CostEstimate(
            flops=int(flops), bytes_accessed=int(moved), transcendentals=0),
    )(scalars, *operands)


class Plan:
    def __init__(self, width):
        self.half = width // CORES
        self.tile = tile_of(self.half, 256)
        self.count = self.half // self.tile
        first = (self.count + 1) // 2
        self.chunks = [(0, first)]
        if self.count > first:
            self.chunks.append((first, self.count - first))


def mask_rows(plan, chunk, scalars, w_down, down_lanes):
    first, steps = chunk
    depth, tile = w_down.shape[1], plan.tile

    def body(_, w_ref, k_ref, out_ref):
        start = pl.program_id(0) * plan.count + first + pl.program_id(1)
        for index in range(tile // BLOCK):
            span = pl.ds(index * BLOCK, BLOCK)
            keep = keep_rows(k_ref, start * (tile // BLOCK) + index, depth)
            out_ref[span, :] = block_rows(w_ref[span, :], keep)

    return call(
        body, (CORES, steps), scalars, (w_down, down_lanes),
        [pl.BlockSpec((tile, depth), lambda h, j, s: (h * plan.count + first + j, 0)),
         whole(down_lanes)],
        pl.BlockSpec((tile, depth), lambda h, j, s: (h * steps + j, 0)),
        jax.ShapeDtypeStruct((CORES * steps * tile, depth), bf16), [],
        0, 4 * CORES * depth * steps * tile)


def gathered(shards, scratch):
    @pl.when(pl.program_id(0) == 0)
    def _():
        row = 0
        for ref in shards:
            scratch[row:row + ref.shape[0], :] = ref[...]
            row += ref.shape[0]


def project(side, plan, chunk, halves, tokens, weights, added=None, inverse_gain=None):
    first, steps = chunk
    local, depth = tokens[0].shape
    rows, tile, count = local * len(tokens), plan.tile, len(tokens)

    def body(_, *refs):
        scratch = refs[-1]
        g_ref, u_ref, gm_ref, um_ref = refs[count:count + 4]
        rest = refs[count + 4:-1]
        gathered(refs[:count], scratch)
        if inverse_gain is not None:
            gain_ref, out_ref, kept_ref, sum_ref = rest

            @pl.when(pl.program_id(0) == 0)
            def _():
                for row in range(0, rows, local):
                    value = scratch[row:row + local, :].astype(f32) * gain_ref[...]
                    sum_ref[row:row + local, :] = jnp.sum(value * value, axis=1, keepdims=True)
        else:
            out_ref, kept_ref = rest[-2:]
        for w_ref, k_ref, lane in ((g_ref, gm_ref, 0), (u_ref, um_ref, tile)):
            for index in range(depth // BLOCK):
                span = pl.ds(index * BLOCK, BLOCK)
                kept_ref[span, lane:lane + tile] = block_rows(
                    w_ref[span, :], keep_rows(k_ref, index, tile))
            value = dot(scratch[...], kept_ref[:, lane:lane + tile], 1, 0)
            if added is not None:
                value += rest[0][:, lane:lane + tile].astype(f32)
            out_ref[:, lane:lane + tile] = value.astype(bf16)

    column = lambda j, h: (0, h[side] * plan.count + first + j)
    weight = pl.BlockSpec((depth, tile), column)
    mask = pl.BlockSpec((depth // BLOCK, tile), column)
    out = pl.BlockSpec((rows, 2 * tile), lambda j, h: (0, j))
    kept = pl.BlockSpec((depth, 2 * tile), lambda j, h: (0, j))
    width = 2 * steps * tile
    extra, extra_specs = [], []
    out_specs = [out, kept]
    shapes = [jax.ShapeDtypeStruct((rows, width), bf16),
              jax.ShapeDtypeStruct((depth, width), bf16)]
    if added is not None:
        extra, extra_specs = [added], [out]
    if inverse_gain is not None:
        extra, extra_specs = [inverse_gain], [whole(inverse_gain)]
        out_specs.append(pl.BlockSpec((rows, 1), lambda j, h: (0, 0)))
        shapes.append(jax.ShapeDtypeStruct((rows, 1), f32))
    return call(
        body, (steps,), halves, (*tokens, *weights, *extra),
        [whole(value) for value in tokens] + [weight, weight, mask, mask] + extra_specs,
        out_specs, shapes, [pltpu.VMEM((rows, depth), bf16)],
        2 * rows * depth * width, 4 * depth * width + 2 * rows * depth + 4 * rows * width)


def back_project(side, halves, tokens, weight, added=None):
    local, depth = tokens[0].shape
    rows, count = local * len(tokens), len(tokens)
    width = weight.shape[0] // CORES
    tile = tile_of(width, 256)
    steps = width // tile

    def body(_, *refs):
        scratch, out_ref, w_ref = refs[-1], refs[-2], refs[count]
        gathered(refs[:count], scratch)
        value = dot(scratch[...], w_ref[...], 1, 1)
        if added is not None:
            value += refs[count + 1][...].astype(f32)
        out_ref[...] = value.astype(bf16)

    out = pl.BlockSpec((rows, tile), lambda i, h: (0, i))
    extra = () if added is None else (added,)
    return call(
        body, (steps,), halves, (*tokens, weight, *extra),
        [whole(value) for value in tokens]
        + [pl.BlockSpec((tile, depth), lambda i, h: (h[side] * steps + i, 0))]
        + [out] * len(extra),
        out, jax.ShapeDtypeStruct((rows, width), bf16), [pltpu.VMEM((rows, depth), bf16)],
        2 * rows * depth * width, 2 * depth * width + 2 * rows * depth + 2 * rows * width)


def activate(plan, scalars, scale, pair, grads, with_hidden):
    rows, width = pair[0].shape
    tile = plan.tile
    count = len(pair)
    operands = [scale, *pair, *(grads or ())]
    in_specs = [whole(scale)]
    in_specs += [pl.BlockSpec((rows, 2 * tile), lambda j, s: (0, j)) for _ in pair]
    in_specs += [pl.BlockSpec((rows, tile), lambda j, s: (0, j)) for _ in grads or ()]
    out_specs, shapes = [], []
    if grads:
        out_specs.append(pl.BlockSpec((rows, 2 * tile), lambda j, s: (0, j)))
        shapes.append(jax.ShapeDtypeStruct((rows, width), bf16))
    if with_hidden:
        out_specs.append(pl.BlockSpec((rows, tile), lambda j, s: (0, j)))
        shapes.append(jax.ShapeDtypeStruct((rows, width // 2), bf16))

    def summed(refs, low, high, lane):
        total = None
        for ref in refs:
            term = ref[low:high, lane:lane + tile].astype(f32)
            total = term if total is None else total + term
        return total

    def body(_, s_ref, *refs):
        outs = refs[len(operands) - 1:]
        for low in range(0, rows, 96 if rows % 96 == 0 else 16):
            high = low + (96 if rows % 96 == 0 else 16)
            factor = s_ref[low:high, :]
            gate = summed(refs[:count], low, high, 0) * factor
            up = summed(refs[:count], low, high, tile) * factor
            sigma = jax.nn.sigmoid(gate)
            silu = gate * sigma
            if grads:
                grad = summed(refs[count:len(operands) - 1], low, high, 0)
                d_gate = grad * up * sigma * (1.0 + gate * (1.0 - sigma))
                outs[0][low:high, :tile] = d_gate.astype(bf16)
                outs[0][low:high, tile:] = (grad * silu).astype(bf16)
            if with_hidden:
                outs[-1][low:high, :] = (silu * up).astype(bf16)

    return call(
        body, (width // 2 // tile,), scalars, operands, in_specs,
        out_specs, shapes, [], 0, 2 * sum(a.size for a in operands) + 3 * rows * width)


def down_product(halves, hidden, weights):
    rows, depth = hidden[0][0].shape[0], weights[0].shape[1]
    tile = tile_of(depth, 256)
    operands, in_specs = [], []
    for pair, weight in zip(hidden, weights):
        width = weight.shape[0] // CORES
        for side, value in enumerate(pair):
            operands += [value, weight]
            in_specs += [whole(value), pl.BlockSpec(
                (width, tile), lambda i, h, side=side: (h[side], i))]

    def body(_, *refs):
        value = None
        for h_ref, w_ref in zip(refs[:-1:2], refs[1:-1:2]):
            term = dot(h_ref[...], w_ref[...], 1, 0)
            value = term if value is None else value + term
        refs[-1][...] = value.astype(bf16)

    total = sum(weight.size for weight in weights)
    return call(
        body, (depth // tile,), halves, operands, in_specs,
        pl.BlockSpec((rows, tile), lambda i, h: (0, i)),
        jax.ShapeDtypeStruct((rows, depth), bf16), [],
        2 * rows * total, 2 * total + 2 * rows * (total // depth + depth))


def input_cotangent(scalars, pair, weights, added, dtype):
    rows = pair[0].shape[0]
    depth, width = weights[0].shape
    tile = tile_of(depth, 256)
    side = pl.BlockSpec((tile, width), lambda i, h: (i, 0))
    extra = () if added is None else (added,)

    def body(_, m_ref, o_ref, wm_ref, wo_ref, *rest):
        value = dot(m_ref[...], wm_ref[...], 1, 1) + dot(o_ref[...], wo_ref[...], 1, 1)
        if added is not None:
            value += rest[0][...]
        rest[-1][...] = value.astype(dtype)

    return call(
        body, (depth // tile,), scalars, (*pair, *weights, *extra),
        [whole(pair[0]), whole(pair[1]), side, side]
        + [pl.BlockSpec((a.shape[0], tile), lambda i, h: (0, i)) for a in extra],
        pl.BlockSpec((rows, tile), lambda i, h: (0, i)),
        jax.ShapeDtypeStruct((rows, depth), dtype), [],
        4 * rows * depth * width, 4 * depth * width + 4 * rows * width + 4 * rows * depth)


def turn(scalars, scale, pieces):
    rows, depth = scale.shape[0], pieces[0].shape[1]
    tile = tile_of(depth, 256)

    def body(_, s_ref, *refs):
        out_ref, scratch = refs[-2:]
        first = 0
        for ref in refs[:-2]:
            span = slice(first, first + ref.shape[0])
            scratch[span, :] = (ref[...].astype(f32) * s_ref[span, :]).astype(bf16)
            first += ref.shape[0]
        out_ref[...] = scratch[...].T

    return call(
        body, (depth // tile,), scalars, (scale, *pieces),
        [whole(scale)] + [pl.BlockSpec((p.shape[0], tile), lambda i, s: (0, i)) for p in pieces],
        pl.BlockSpec((tile, rows), lambda i, s: (i, 0)),
        jax.ShapeDtypeStruct((depth, rows), bf16), [pltpu.VMEM((rows, tile), bf16)],
        0, 4 * rows * depth)


def gate_up_grads(plan, chunk, halves, turned, mine, other, gate_lanes, up_lanes, earlier,
                  single=None):
    first, steps = chunk
    skipped = 0
    if single is not None:
        first, steps, skipped = first + single, 1, single
    depth, rows = turned.shape
    tile = plan.tile
    n_mine = len(mine)

    def body(_, x_ref, *refs):
        sides = refs[:n_mine], refs[n_mine:2 * n_mine]
        masks = refs[2 * n_mine:2 * n_mine + 2]
        outs, scratch = refs[-3:-1], refs[-1]

        def collect(pieces):
            row = 0
            for ref in pieces:
                scratch[row:row + ref.shape[0], :] = ref[...]
                row += ref.shape[0]

        pl.when(pl.program_id(0) == 0)(lambda: collect(sides[0]))
        pl.when(pl.program_id(0) == 1)(lambda: collect(sides[1]))
        for index in range(2):
            right = scratch[:, index * tile:(index + 1) * tile]
            value = dot(x_ref[...], right, 1, 0).astype(bf16)
            for block in range(depth // BLOCK):
                span = slice(block * BLOCK, (block + 1) * BLOCK)
                outs[index][span, :] = block_rows(
                    value[span, :], keep_rows(masks[index], block, tile))

    column = lambda p, j, h: (0, h[p] * plan.count + first + j)
    in_specs = [whole(turned)]
    in_specs += [pl.BlockSpec((a.shape[0], 2 * tile), lambda p, j, h: (
        0, skipped + jnp.where(p == 0, j, steps - 1))) for a in mine]
    in_specs += [pl.BlockSpec((a.shape[0], 2 * tile), lambda p, j, h: (
        0, skipped + jnp.where(p == 0, 0, j))) for a in other]
    in_specs += [pl.BlockSpec((depth // BLOCK, tile), column)] * 2
    out = pl.BlockSpec((depth, tile), column)
    shape = jax.ShapeDtypeStruct((depth, plan.half * CORES), bf16)
    operands = [turned, *mine, *other, gate_lanes, up_lanes]
    aliases = None
    if earlier is not None:
        aliases = {len(operands) + 1: 0, len(operands) + 2: 1}
        operands += earlier
        in_specs += [pl.BlockSpec(memory_space=pl.ANY)] * 2
    return call(
        body, (CORES, steps), halves, operands, in_specs, [out, out], [shape, shape],
        [pltpu.VMEM((rows, 2 * tile), bf16)],
        8 * rows * depth * steps * tile,
        2 * rows * depth + 8 * rows * steps * tile + 8 * depth * steps * tile, aliases)


def down_grads(plan, halves, hidden, grads, down_lanes):
    rows, depth = hidden[0][0].shape[0], grads[0].shape[1]
    tile = tile_of(depth, 256)
    operands, places = [], []
    for pair, (first, steps) in zip(hidden, plan.chunks):
        for side, value in enumerate(pair):
            operands.append(value)
            places.append((side, first * plan.tile))
    count = len(operands)
    width = plan.half * CORES

    def body(half_ref, *refs):
        turned, right, out_ref = refs[-2], refs[-1], refs[-3]

        @pl.when(pl.program_id(0) == 0)
        def _():
            for ref, (side, first) in zip(refs[:count], places):
                start = pl.multiple_of(half_ref[side] * plan.half + first, 128)
                for lane in range(0, ref.shape[1], plan.tile):
                    turned[pl.ds(start + lane, plan.tile), :] = ref[:, lane:lane + plan.tile].T

        row = 0
        for ref in refs[count:count + len(grads)]:
            right[row:row + ref.shape[0], :] = ref[...]
            row += ref.shape[0]
        k_ref = refs[count + len(grads)]
        piece = plan.tile
        for part in range(width // piece):
            value = dot(turned[part * piece:(part + 1) * piece, :], right[...], 1, 0).astype(bf16)
            for block in range(piece // BLOCK):
                low = part * piece + block * BLOCK
                out_ref[low:low + BLOCK, :] = block_rows(
                    value[block * BLOCK:(block + 1) * BLOCK, :],
                    keep_rows(k_ref, low // BLOCK, tile))

    column = lambda i, h: (0, i)
    return call(
        body, (depth // tile,), halves, (*operands, *grads, down_lanes),
        [whole(value) for value in operands]
        + [pl.BlockSpec((g.shape[0], tile), column) for g in grads]
        + [pl.BlockSpec((down_lanes.shape[0], tile), column)],
        pl.BlockSpec((width, tile), column),
        jax.ShapeDtypeStruct((width, depth), bf16),
        [pltpu.VMEM((width, rows), bf16), pltpu.VMEM((rows, tile), bf16)],
        2 * rows * depth * width, 2 * depth * width + 2 * rows * width + 2 * rows * depth)


def after(value, *others):
    return lax.optimization_barrier((value, *others))[0]


def shards(n_row, n_col, inputs, norm_gain, w_gate, w_up, w_down,
           mask_gate, mask_up, mask_down, grad_out):
    n_chip = n_col // CORES
    local, width = inputs.shape
    features = width * n_col
    plan = Plan(w_gate.shape[1])
    chunks = plan.chunks
    cycle = list(range(0, n_row, 2)) + list(range(n_row - 1, 0, -2))
    ahead = [(cycle[i], cycle[(i + 1) % n_row]) for i in range(n_row)]
    behind = [(b, a) for a, b in ahead]
    swap = [(i, i ^ 1) for i in range(n_col)]
    n_ahead, n_behind = n_row // 2, (n_row - 1) // 2

    def to_partner(value):
        return lax.ppermute(value, "col", swap)

    def from_chips(value):
        return [
            lax.ppermute(value, "col", [(i, (i + CORES * k) % n_col) for i in range(n_col)])
            for k in range(1, n_chip)
        ]

    def total_over_chips(value):
        total = value
        for other in from_chips(value):
            total = total + other
        return total

    offsets = [0]
    for k in range(1, n_ahead + 1):
        offsets.append(-k)
        if k <= n_behind:
            offsets.append(k)

    core = lax.rem(lax.axis_index("col"), CORES).astype(jnp.int32)
    halves = jnp.stack([core, 1 - core])

    inputs_wide = inputs.astype(f32)
    scaled = (inputs_wide * norm_gain).astype(bf16)

    def ring_step(found, k, *ready):
        found[-k] = lax.ppermute(after(found[1 - k], *ready), "row", ahead)
        if k <= n_behind:
            found[k] = lax.ppermute(after(found[k - 1], *ready), "row", behind)

    shard = {0: scaled}
    ring_step(shard, 1)
    down_lanes = lanes(mask_down)
    dn = [mask_rows(plan, chunks[0], halves, w_down, down_lanes)]
    ring_step(shard, 2, dn[0])
    dn.append(mask_rows(plan, chunks[1], after(halves, dn[0]), w_down, down_lanes))
    ring_step(shard, 3, dn[1])
    gate_lanes = lanes(after(mask_gate, dn[1]))
    up_lanes = lanes(after(mask_up, dn[1]))
    for k in range(4, n_ahead + 1):
        ring_step(shard, k, gate_lanes, up_lanes)
    tokens = [shard[offset] for offset in offsets]
    weights = (w_gate, w_up, gate_lanes, up_lanes)

    sent0, kept0_o, squares = project(
        1, plan, chunks[0], halves, tokens, weights,
        inverse_gain=(1.0 / norm_gain)[None])
    grad_shard = {0: after(grad_out, *tokens)}
    ring_step(grad_shard, 1)
    squares = squares[:, 0]
    squares = squares + to_partner(squares)
    got0 = to_partner(sent0)
    own0, kept0_m = project(
        0, plan, chunks[0], after(halves, sent0), tokens, weights, got0)
    others = from_chips(squares)
    for other in others:
        squares = squares + other
    scale = lax.rsqrt(squares / features + epsilon)[:, None]
    others0 = from_chips(after(own0, *others))

    ring_step(grad_shard, 2, own0)
    sent1, kept1_o = project(1, plan, chunks[1], after(halves, own0), tokens, weights)
    ring_step(grad_shard, 3, sent1)
    turned = turn(after(halves, sent1), scale, tokens)
    for k in range(4, n_ahead + 1):
        ring_step(grad_shard, k, turned)
    own1, kept1_m = project(
        0, plan, chunks[1], after(halves, turned), tokens, weights, to_partner(sent1))
    grads = [grad_shard[offset] for offset in offsets]
    sent_b0 = back_project(1, after(halves, own1), grads, dn[0])
    sent_b1 = back_project(1, after(halves, sent_b0), grads, dn[1])
    got_b1 = to_partner(sent_b1)
    own_b0 = back_project(0, after(halves, sent_b1), grads, dn[0], to_partner(sent_b0))
    others_b0 = from_chips(after(own_b0, *others0))
    own_b1 = back_project(0, after(halves, own_b0), grads, dn[1], got_b1)
    others1 = from_chips(after(own1, *others_b0))
    cot0, hidden0 = activate(plan, after(halves, own_b1), scale, [own0, *others0],
                             [own_b0, *others_b0], True)
    cot0 = (cot0, to_partner(cot0))
    hidden0 = (hidden0, to_partner(hidden0))
    partial = input_cotangent(halves, cot0, (kept0_m, kept0_o), None, f32)
    grad_gu = gate_up_grads(plan, chunks[0], after(halves, partial), turned,
                            cot0[:1], cot0[1:], gate_lanes, up_lanes, None)

    others_b1 = from_chips(after(own_b1, *others1))
    hidden1, = activate(plan, after(halves, grad_gu[0]), scale, [own1, *others1],
                        None, True)
    hidden1 = (hidden1, to_partner(hidden1))
    mixed = down_product(halves, (hidden0, hidden1), dn)

    def scatter(parts):
        back = parts(-n_ahead)
        front = parts(n_behind)
        for k in range(1, n_ahead + 1):
            back = lax.ppermute(back, "row", behind)
            if k < n_ahead:
                back = (back.astype(f32) + parts(k - n_ahead).astype(f32)).astype(bf16)
            if k <= n_behind:
                front = lax.ppermute(front, "row", ahead)
                if k < n_behind:
                    front = (front.astype(f32) + parts(n_behind - k).astype(f32)).astype(bf16)
        return back.astype(f32) + front.astype(f32) + parts(0).astype(f32)

    def part_of(value):
        parts = {offset: lax.slice_in_dim(value, i * local, (i + 1) * local, axis=0)
                 for i, offset in enumerate(offsets)}
        return lambda offset: parts[offset]

    output = (inputs_wide + scatter(part_of(mixed))).astype(bf16)
    cot1, = activate(plan, after(halves, mixed), scale, [own1, *others1],
                     [own_b1, *others_b1], False)
    cot1 = (cot1, to_partner(cot1))
    norm_all = input_cotangent(halves, cot1, (kept1_m, kept1_o), partial, bf16)
    d_norm_in = scatter(part_of(norm_all))
    grad_w_down = down_grads(plan, after(halves, norm_all), (hidden0, hidden1),
                             grads, down_lanes)
    ready = grad_w_down
    for index in range(chunks[1][1]):
        grad_gu = gate_up_grads(
            plan, chunks[1], after(halves, ready), turned,
            cot1[:1], cot1[1:], gate_lanes, up_lanes, grad_gu, index)
        ready = grad_gu[0]
    grad_w_gate, grad_w_up = grad_gu

    inv_local = scale[:local]
    normed = inputs_wide * inv_local
    d_normed = d_norm_in * norm_gain
    inner = jnp.sum(d_normed * normed, axis=1)
    inner = inner + to_partner(inner)
    inner = total_over_chips(inner) / features
    gain_part = jnp.sum(d_norm_in * normed, axis=0)
    step = 1
    while step < n_row:
        gain_part = gain_part + lax.ppermute(
            gain_part, "row", [(i, i ^ step) for i in range(n_row)])
        step *= 2
    grad_inputs = (
        grad_out.astype(f32) + inv_local * (d_normed - normed * inner[:, None])
    ).astype(bf16)
    return (output, grad_inputs, gain_part, grad_w_gate, grad_w_up, grad_w_down)


def solution(mesh):
    in_specs = (
        P("row", "col"),
        P("col"),
        P("col", "row"),
        P("col", "row"),
        P("row", "col"),
        P("col", "row"),
        P("col", "row"),
        P("row", "col"),
        P("row", "col"),
    )
    out_specs = (
        P("row", "col"),
        P("row", "col"),
        P("col"),
        P("col", "row"),
        P("col", "row"),
        P("row", "col"),
    )
    body = functools.partial(shards, mesh.shape["row"], mesh.shape["col"])

    return jax.shard_map(
        body, mesh=mesh, in_specs=in_specs, out_specs=out_specs, check_vma=False)
```

```python
import functools

import jax
import jax.numpy as jnp
from jax import lax
from jax.experimental import pallas as pl
from jax.experimental.pallas import tpu as pltpu
from jax.sharding import PartitionSpec as P

BLOCK = 64
CORES = 2
epsilon = 1e-05
bf16 = jnp.bfloat16
f32 = jnp.float32


def tile_of(size, limit):
    best = 128
    for tile in range(128, limit + 1, 128):
        if size % tile == 0:
            best = tile
    return best


def lanes(block_mask):
    rows, cols = block_mask.shape
    wide = jnp.broadcast_to(block_mask.astype(f32)[:, :, None], (rows, cols, BLOCK))
    return lax.optimization_barrier(wide.reshape(rows, cols * BLOCK))


def dot(left, right, left_axis, right_axis):
    return lax.dot_general(
        left, right, (((left_axis,), (right_axis,)), ((), ())), preferred_element_type=f32
    )


def keep_rows(mask_ref, row, cols):
    keep = jnp.broadcast_to(mask_ref[pl.ds(row, 1), :], (16, cols))
    return keep.astype(bf16)[None]


def block_rows(value, keep):
    cols = value.shape[1]
    return (value.reshape(BLOCK // 16, 16, cols) * keep).reshape(BLOCK, cols)


def whole(array):
    return pl.BlockSpec(array.shape, lambda *_: (0,) * array.ndim)


def call(body, grid, scalars, operands, in_specs, out_specs, out_shape, scratch,
         flops, moved, aliases=None):
    return pl.pallas_call(
        body,
        grid_spec=pltpu.PrefetchScalarGridSpec(
            num_scalar_prefetch=1,
            grid=grid,
            in_specs=in_specs,
            out_specs=out_specs,
            scratch_shapes=scratch,
        ),
        out_shape=out_shape,
        input_output_aliases=aliases or {},
        compiler_params=pltpu.CompilerParams(vmem_limit_bytes=60 << 20),
        cost_estimate=pl.CostEstimate(
            flops=int(flops), bytes_accessed=int(moved), transcendentals=0),
    )(scalars, *operands)


class Plan:
    def __init__(self, width):
        self.half = width // CORES
        self.tile = tile_of(self.half, 256)
        self.count = self.half // self.tile
        first = (self.count + 1) // 2
        self.chunks = [(0, first)]
        if self.count > first:
            self.chunks.append((first, self.count - first))


def chunk_tile(chunk):
    first, steps = chunk
    return steps, lambda j: jnp.clip(j - first, 0, steps - 1)


def mask_rows(plan, scalars, w_down, down_lanes):
    depth, tile = w_down.shape[1], plan.tile

    def body(_, w_ref, k_ref, *outs):
        half, step = pl.program_id(0), pl.program_id(1)
        start = half * plan.count + step
        for (first, steps), out_ref in zip(plan.chunks, outs):
            @pl.when(jnp.logical_and(step >= first, step < first + steps))
            def _(out_ref=out_ref):
                for index in range(tile // BLOCK):
                    span = pl.ds(index * BLOCK, BLOCK)
                    keep = keep_rows(k_ref, start * (tile // BLOCK) + index, depth)
                    out_ref[span, :] = block_rows(w_ref[span, :], keep)

    out_specs, shapes = [], []
    for chunk in plan.chunks:
        steps, local = chunk_tile(chunk)
        out_specs.append(pl.BlockSpec(
            (tile, depth), lambda h, j, s, n=steps, f=local: (h * n + f(j), 0)))
        shapes.append(jax.ShapeDtypeStruct((CORES * steps * tile, depth), bf16))
    return call(
        body, (CORES, plan.count), scalars, (w_down, down_lanes),
        [pl.BlockSpec((tile, depth), lambda h, j, s: (h * plan.count + j, 0)),
         whole(down_lanes)],
        out_specs, shapes, [], 0, 4 * w_down.size)


def gathered(shards, scratch):
    @pl.when(pl.program_id(0) == 0)
    def _():
        row = 0
        for ref in shards:
            scratch[row:row + ref.shape[0], :] = ref[...]
            row += ref.shape[0]


def project(side, plan, chunk, halves, tokens, weights, added=None, inverse_gain=None):
    first, steps = chunk
    local, depth = tokens[0].shape
    rows, tile, count = local * len(tokens), plan.tile, len(tokens)

    def body(_, *refs):
        scratch = refs[-1]
        g_ref, u_ref, gm_ref, um_ref = refs[count:count + 4]
        rest = refs[count + 4:-1]
        gathered(refs[:count], scratch)
        if inverse_gain is not None:
            gain_ref, out_ref, kept_ref, sum_ref = rest

            @pl.when(pl.program_id(0) == 0)
            def _():
                for row in range(0, rows, local):
                    value = scratch[row:row + local, :].astype(f32) * gain_ref[...]
                    sum_ref[row:row + local, :] = jnp.sum(value * value, axis=1, keepdims=True)
        else:
            out_ref, kept_ref = rest[-2:]
        for w_ref, k_ref, lane in ((g_ref, gm_ref, 0), (u_ref, um_ref, tile)):
            for index in range(depth // BLOCK):
                span = pl.ds(index * BLOCK, BLOCK)
                kept_ref[span, lane:lane + tile] = block_rows(
                    w_ref[span, :], keep_rows(k_ref, index, tile))
            value = dot(scratch[...], kept_ref[:, lane:lane + tile], 1, 0)
            if added is not None:
                value += rest[0][:, lane:lane + tile].astype(f32)
            out_ref[:, lane:lane + tile] = value.astype(bf16)

    column = lambda j, h: (0, h[side] * plan.count + first + j)
    weight = pl.BlockSpec((depth, tile), column)
    mask = pl.BlockSpec((depth // BLOCK, tile), column)
    out = pl.BlockSpec((rows, 2 * tile), lambda j, h: (0, j))
    kept = pl.BlockSpec((depth, 2 * tile), lambda j, h: (0, j))
    width = 2 * steps * tile
    extra, extra_specs = [], []
    out_specs = [out, kept]
    shapes = [jax.ShapeDtypeStruct((rows, width), bf16),
              jax.ShapeDtypeStruct((depth, width), bf16)]
    if added is not None:
        extra, extra_specs = [added], [out]
    if inverse_gain is not None:
        extra, extra_specs = [inverse_gain], [whole(inverse_gain)]
        out_specs.append(pl.BlockSpec((rows, 1), lambda j, h: (0, 0)))
        shapes.append(jax.ShapeDtypeStruct((rows, 1), f32))
    return call(
        body, (steps,), halves, (*tokens, *weights, *extra),
        [whole(value) for value in tokens] + [weight, weight, mask, mask] + extra_specs,
        out_specs, shapes, [pltpu.VMEM((rows, depth), bf16)],
        2 * rows * depth * width, 4 * depth * width + 2 * rows * depth + 4 * rows * width)


def back_project(side, plan, halves, tokens, weights, added=None):
    local, depth = tokens[0].shape
    rows, count, tile = local * len(tokens), len(tokens), plan.tile
    parts = len(plan.chunks)

    def body(_, *refs):
        scratch = refs[-1]
        gathered(refs[:count], scratch)
        w_refs = refs[count:count + parts]
        rest = refs[count + parts:-1]
        outs = rest if added is None else rest[1:]
        step = pl.program_id(0)
        for index, (first, steps) in enumerate(plan.chunks):
            @pl.when(jnp.logical_and(step >= first, step < first + steps))
            def _(w_ref=w_refs[index], out_ref=outs[index if len(outs) > 1 else 0]):
                value = dot(scratch[...], w_ref[...], 1, 1)
                if added is not None:
                    value += rest[0][...].astype(f32)
                out_ref[...] = value.astype(bf16)

    in_specs = [whole(value) for value in tokens]
    out = pl.BlockSpec((rows, tile), lambda j, h: (0, j))
    out_specs, shapes = [], []
    for chunk in plan.chunks:
        steps, place = chunk_tile(chunk)
        in_specs.append(pl.BlockSpec(
            (tile, depth), lambda j, h, n=steps, f=place: (h[side] * n + f(j), 0)))
        out_specs.append(pl.BlockSpec((rows, tile), lambda j, h, f=place: (0, f(j))))
        shapes.append(jax.ShapeDtypeStruct((rows, steps * tile), bf16))
    extra = ()
    if added is None:
        out_specs, shapes = [out], [jax.ShapeDtypeStruct((rows, plan.half), bf16)]
    else:
        extra = (added,)
        in_specs.append(out)
    return call(
        body, (plan.count,), halves, (*tokens, *weights, *extra), in_specs,
        out_specs, shapes, [pltpu.VMEM((rows, depth), bf16)],
        2 * rows * depth * plan.half,
        2 * depth * plan.half + 2 * rows * depth + 2 * rows * plan.half)


def activate(plan, scalars, scale, pair, grads, with_hidden):
    rows, width = pair[0].shape
    tile = plan.tile
    count = len(pair)
    operands = [scale, *pair, *(grads or ())]
    in_specs = [whole(scale)]
    in_specs += [pl.BlockSpec((rows, 2 * tile), lambda j, s: (0, j)) for _ in pair]
    in_specs += [pl.BlockSpec((rows, tile), lambda j, s: (0, j)) for _ in grads or ()]
    out_specs, shapes = [], []
    if grads:
        out_specs.append(pl.BlockSpec((rows, 2 * tile), lambda j, s: (0, j)))
        shapes.append(jax.ShapeDtypeStruct((rows, width), bf16))
    if with_hidden:
        out_specs.append(pl.BlockSpec((rows, tile), lambda j, s: (0, j)))
        shapes.append(jax.ShapeDtypeStruct((rows, width // 2), bf16))

    def summed(refs, low, high, lane):
        total = None
        for ref in refs:
            term = ref[low:high, lane:lane + tile].astype(f32)
            total = term if total is None else total + term
        return total

    def body(_, s_ref, *refs):
        outs = refs[len(operands) - 1:]
        for low in range(0, rows, 96 if rows % 96 == 0 else 16):
            high = low + (96 if rows % 96 == 0 else 16)
            factor = s_ref[low:high, :]
            gate = summed(refs[:count], low, high, 0) * factor
            up = summed(refs[:count], low, high, tile) * factor
            sigma = jax.nn.sigmoid(gate)
            silu = gate * sigma
            if grads:
                grad = summed(refs[count:len(operands) - 1], low, high, 0)
                d_gate = grad * up * sigma * (1.0 + gate * (1.0 - sigma))
                outs[0][low:high, :tile] = d_gate.astype(bf16)
                outs[0][low:high, tile:] = (grad * silu).astype(bf16)
            if with_hidden:
                outs[-1][low:high, :] = (silu * up).astype(bf16)

    return call(
        body, (width // 2 // tile,), scalars, operands, in_specs,
        out_specs, shapes, [], 0, 2 * sum(a.size for a in operands) + 3 * rows * width)


def down_product(halves, pair, weight, added, dtype):
    rows, width = pair[0].shape
    depth = weight.shape[1]
    tile = tile_of(depth, 256)
    out = pl.BlockSpec((rows, tile), lambda i, h: (0, i))
    extra = () if added is None else (added,)

    def body(_, m_ref, o_ref, wm_ref, wo_ref, *rest):
        value = dot(m_ref[...], wm_ref[...], 1, 0) + dot(o_ref[...], wo_ref[...], 1, 0)
        if added is not None:
            value += rest[0][...]
        rest[-1][...] = value.astype(dtype)

    return call(
        body, (depth // tile,), halves, (*pair, weight, weight, *extra),
        [whole(pair[0]), whole(pair[1]),
         pl.BlockSpec((width, tile), lambda i, h: (h[0], i)),
         pl.BlockSpec((width, tile), lambda i, h: (h[1], i))] + [out] * len(extra),
        out, jax.ShapeDtypeStruct((rows, depth), dtype), [],
        2 * rows * weight.size, 2 * weight.size + 4 * rows * width + 4 * rows * depth)


def input_cotangent(scalars, pair, weights, added, dtype):
    rows = pair[0].shape[0]
    depth, width = weights[0].shape
    tile = tile_of(depth, 256)
    side = pl.BlockSpec((tile, width), lambda i, h: (i, 0))
    extra = () if added is None else (added,)

    def body(_, m_ref, o_ref, wm_ref, wo_ref, *rest):
        value = dot(m_ref[...], wm_ref[...], 1, 1) + dot(o_ref[...], wo_ref[...], 1, 1)
        if added is not None:
            value += rest[0][...]
        rest[-1][...] = value.astype(dtype)

    return call(
        body, (depth // tile,), scalars, (*pair, *weights, *extra),
        [whole(pair[0]), whole(pair[1]), side, side]
        + [pl.BlockSpec((a.shape[0], tile), lambda i, h: (0, i)) for a in extra],
        pl.BlockSpec((rows, tile), lambda i, h: (0, i)),
        jax.ShapeDtypeStruct((rows, depth), dtype), [],
        4 * rows * depth * width, 4 * depth * width + 4 * rows * width + 4 * rows * depth)


def turn(scalars, scale, pieces):
    rows, depth = scale.shape[0], pieces[0].shape[1]
    tile = tile_of(depth, 256)

    def body(_, s_ref, *refs):
        out_ref, scratch = refs[-2:]
        first = 0
        for ref in refs[:-2]:
            span = slice(first, first + ref.shape[0])
            scratch[span, :] = (ref[...].astype(f32) * s_ref[span, :]).astype(bf16)
            first += ref.shape[0]
        out_ref[...] = scratch[...].T

    return call(
        body, (depth // tile,), scalars, (scale, *pieces),
        [whole(scale)] + [pl.BlockSpec((p.shape[0], tile), lambda i, s: (0, i)) for p in pieces],
        pl.BlockSpec((tile, rows), lambda i, s: (i, 0)),
        jax.ShapeDtypeStruct((depth, rows), bf16), [pltpu.VMEM((rows, tile), bf16)],
        0, 4 * rows * depth)


def gate_up_grads(plan, chunk, halves, turned, mine, other, gate_lanes, up_lanes, earlier,
                  single=None):
    first, steps = chunk
    skipped = 0
    if single is not None:
        first, steps, skipped = first + single, 1, single
    depth, rows = turned.shape
    tile = plan.tile
    n_mine = len(mine)

    def body(_, x_ref, *refs):
        sides = refs[:n_mine], refs[n_mine:2 * n_mine]
        masks = refs[2 * n_mine:2 * n_mine + 2]
        outs, scratch = refs[-3:-1], refs[-1]

        def collect(pieces):
            row = 0
            for ref in pieces:
                scratch[row:row + ref.shape[0], :] = ref[...]
                row += ref.shape[0]

        pl.when(pl.program_id(0) == 0)(lambda: collect(sides[0]))
        pl.when(pl.program_id(0) == 1)(lambda: collect(sides[1]))
        for index in range(2):
            right = scratch[:, index * tile:(index + 1) * tile]
            value = dot(x_ref[...], right, 1, 0).astype(bf16)
            for block in range(depth // BLOCK):
                span = slice(block * BLOCK, (block + 1) * BLOCK)
                outs[index][span, :] = block_rows(
                    value[span, :], keep_rows(masks[index], block, tile))

    column = lambda p, j, h: (0, h[p] * plan.count + first + j)
    in_specs = [whole(turned)]
    in_specs += [pl.BlockSpec((a.shape[0], 2 * tile), lambda p, j, h: (
        0, skipped + jnp.where(p == 0, j, steps - 1))) for a in mine]
    in_specs += [pl.BlockSpec((a.shape[0], 2 * tile), lambda p, j, h: (
        0, skipped + jnp.where(p == 0, 0, j))) for a in other]
    in_specs += [pl.BlockSpec((depth // BLOCK, tile), column)] * 2
    out = pl.BlockSpec((depth, tile), column)
    shape = jax.ShapeDtypeStruct((depth, plan.half * CORES), bf16)
    operands = [turned, *mine, *other, gate_lanes, up_lanes]
    aliases = None
    if earlier is not None:
        aliases = {len(operands) + 1: 0, len(operands) + 2: 1}
        operands += earlier
        in_specs += [pl.BlockSpec(memory_space=pl.ANY)] * 2
    return call(
        body, (CORES, steps), halves, operands, in_specs, [out, out], [shape, shape],
        [pltpu.VMEM((rows, 2 * tile), bf16)],
        8 * rows * depth * steps * tile,
        2 * rows * depth + 8 * rows * steps * tile + 8 * depth * steps * tile, aliases)


def down_grads(plan, chunk, halves, pair, grads, down_lanes, earlier):
    first, steps = chunk
    local, depth = grads[0].shape
    count, tile = len(grads), plan.tile
    rows = local * count

    def body(half_ref, *refs):
        right, left = refs[-2:]
        gathered(refs[:count], right)
        m_ref, o_ref, k_ref, out_ref = refs[count], refs[count + 1], refs[count + 2], refs[-3]

        @pl.when(pl.program_id(0) == 0)
        def _():
            left[...] = m_ref[...].T

        @pl.when(pl.program_id(0) == 1)
        def _():
            left[...] = o_ref[...].T

        value = dot(left[...], right[...], 1, 0).astype(bf16)
        start = half_ref[pl.program_id(0)] * plan.count + first + pl.program_id(1)
        for block in range(tile // BLOCK):
            span = slice(block * BLOCK, (block + 1) * BLOCK)
            out_ref[span, :] = block_rows(
                value[span, :], keep_rows(k_ref, start * (tile // BLOCK) + block, depth))

    operands = [*grads, *pair, down_lanes]
    in_specs = [whole(g) for g in grads] + [
        pl.BlockSpec((rows, tile), lambda p, j, h: (0, jnp.where(p == 0, j, steps - 1))),
        pl.BlockSpec((rows, tile), lambda p, j, h: (0, jnp.where(p == 0, 0, j))),
        whole(down_lanes)]
    aliases = None
    if earlier is not None:
        aliases = {len(operands) + 1: 0}
        operands.append(earlier)
        in_specs.append(pl.BlockSpec(memory_space=pl.ANY))
    return call(
        body, (CORES, steps), halves, operands, in_specs,
        pl.BlockSpec((tile, depth), lambda p, j, h: (h[p] * plan.count + first + j, 0)),
        jax.ShapeDtypeStruct((CORES * plan.half, depth), bf16),
        [pltpu.VMEM((rows, depth), bf16), pltpu.VMEM((tile, rows), bf16)],
        4 * rows * depth * steps * tile,
        4 * depth * steps * tile + 4 * rows * steps * tile + 2 * rows * depth, aliases)


def after(value, *others):
    return lax.optimization_barrier((value, *others))[0]


def shards(n_row, n_col, inputs, norm_gain, w_gate, w_up, w_down,
           mask_gate, mask_up, mask_down, grad_out):
    n_chip = n_col // CORES
    local, width = inputs.shape
    features = width * n_col
    plan = Plan(w_gate.shape[1])
    chunks = plan.chunks
    cycle = list(range(0, n_row, 2)) + list(range(n_row - 1, 0, -2))
    ahead = [(cycle[i], cycle[(i + 1) % n_row]) for i in range(n_row)]
    behind = [(b, a) for a, b in ahead]
    swap = [(i, i ^ 1) for i in range(n_col)]
    n_ahead, n_behind = n_row // 2, (n_row - 1) // 2

    def to_partner(value):
        return lax.ppermute(value, "col", swap)

    def from_chips(value):
        return [
            lax.ppermute(value, "col", [(i, (i + CORES * k) % n_col) for i in range(n_col)])
            for k in range(1, n_chip)
        ]

    def total_over_chips(value):
        total = value
        for other in from_chips(value):
            total = total + other
        return total

    offsets = [0]
    for k in range(1, n_ahead + 1):
        offsets.append(-k)
        if k <= n_behind:
            offsets.append(k)

    core = lax.rem(lax.axis_index("col"), CORES).astype(jnp.int32)
    halves = jnp.stack([core, 1 - core])

    inputs_wide = inputs.astype(f32)
    scaled = (inputs_wide * norm_gain).astype(bf16)

    def ring_step(found, k, *ready):
        found[-k] = lax.ppermute(after(found[1 - k], *ready), "row", ahead)
        if k <= n_behind:
            found[k] = lax.ppermute(after(found[k - 1], *ready), "row", behind)

    shard = {0: scaled}
    ring_step(shard, 1)
    down_lanes = lanes(mask_down)
    gate_lanes = lanes(mask_gate)
    up_lanes = lanes(mask_up)
    ring_step(shard, 2, gate_lanes, up_lanes)
    dn = mask_rows(plan, after(halves, shard[-1]), w_down, down_lanes)
    ring_step(shard, 3, dn[0])
    for k in range(4, n_ahead + 1):
        ring_step(shard, k)
    tokens = [shard[offset] for offset in offsets]
    weights = (w_gate, w_up, gate_lanes, up_lanes)

    sent0, kept0_o, squares = project(
        1, plan, chunks[0], halves, tokens, weights,
        inverse_gain=(1.0 / norm_gain)[None])
    grad_shard = {0: after(grad_out, *tokens)}
    ring_step(grad_shard, 1)
    squares = squares[:, 0]
    squares = squares + to_partner(squares)
    got0 = to_partner(sent0)
    own0, kept0_m = project(
        0, plan, chunks[0], after(halves, sent0), tokens, weights, got0)
    others = from_chips(squares)
    for other in others:
        squares = squares + other
    scale = lax.rsqrt(squares / features + epsilon)[:, None]
    others0 = from_chips(after(own0, *others))

    ring_step(grad_shard, 2, own0)
    sent1, kept1_o = project(1, plan, chunks[1], after(halves, own0), tokens, weights)
    ring_step(grad_shard, 3, sent1)
    turned = turn(after(halves, sent1), scale, tokens)
    for k in range(4, n_ahead + 1):
        ring_step(grad_shard, k, turned)
    own1, kept1_m = project(
        0, plan, chunks[1], after(halves, turned), tokens, weights, to_partner(sent1))
    grads = [grad_shard[offset] for offset in offsets]
    sent_b, = back_project(1, plan, after(halves, own1), grads, dn)
    own_b0, own_b1 = back_project(
        0, plan, halves, grads, dn, to_partner(sent_b))
    others_b0 = from_chips(after(own_b0, *others0))
    others1 = from_chips(after(own1, *others_b0))
    hidden0, = activate(plan, after(halves, own_b1), scale, [own0, *others0], None, True)
    hidden0 = (hidden0, to_partner(hidden0))
    mixed = down_product(halves, hidden0, dn[0], None, f32)
    grad_w_down = down_grads(plan, chunks[0], after(halves, mixed), hidden0, grads,
                             down_lanes, None)
    halves = after(halves, grad_w_down)
    cot0, = activate(plan, halves, scale, [own0, *others0], [own_b0, *others_b0], False)
    cot0 = (cot0, to_partner(cot0))
    partial = input_cotangent(halves, cot0, (kept0_m, kept0_o), None, f32)
    grad_gu = gate_up_grads(plan, chunks[0], after(halves, partial), turned,
                            cot0[:1], cot0[1:], gate_lanes, up_lanes, None)

    others_b1 = from_chips(after(own_b1, *others1))
    hidden1, = activate(plan, after(halves, grad_gu[0]), scale, [own1, *others1],
                        None, True)
    hidden1 = (hidden1, to_partner(hidden1))
    mixed = down_product(halves, hidden1, dn[1], mixed, bf16)
    grad_w_down = down_grads(plan, chunks[1], after(halves, mixed), hidden1, grads,
                             down_lanes, grad_w_down)

    def scatter(parts):
        back = parts(-n_ahead)
        front = parts(n_behind)
        for k in range(1, n_ahead + 1):
            back = lax.ppermute(back, "row", behind)
            if k < n_ahead:
                back = (back.astype(f32) + parts(k - n_ahead).astype(f32)).astype(bf16)
            if k <= n_behind:
                front = lax.ppermute(front, "row", ahead)
                if k < n_behind:
                    front = (front.astype(f32) + parts(n_behind - k).astype(f32)).astype(bf16)
        return back.astype(f32) + front.astype(f32) + parts(0).astype(f32)

    def part_of(value):
        parts = {offset: lax.slice_in_dim(value, i * local, (i + 1) * local, axis=0)
                 for i, offset in enumerate(offsets)}
        return lambda offset: parts[offset]

    output = (inputs_wide + scatter(part_of(mixed))).astype(bf16)
    cot1, = activate(plan, after(halves, grad_w_down), scale, [own1, *others1],
                     [own_b1, *others_b1], False)
    cot1 = (cot1, to_partner(cot1))
    norm_all = input_cotangent(halves, cot1, (kept1_m, kept1_o), partial, bf16)
    d_norm_in = scatter(part_of(norm_all))
    ready = norm_all
    for index in range(chunks[1][1]):
        grad_gu = gate_up_grads(
            plan, chunks[1], after(halves, ready), turned,
            cot1[:1], cot1[1:], gate_lanes, up_lanes, grad_gu, index)
        ready = grad_gu[0]
    grad_w_gate, grad_w_up = grad_gu

    inv_local = scale[:local]
    normed = inputs_wide * inv_local
    d_normed = d_norm_in * norm_gain
    inner = jnp.sum(d_normed * normed, axis=1)
    inner = inner + to_partner(inner)
    inner = total_over_chips(inner) / features
    gain_part = jnp.sum(d_norm_in * normed, axis=0)
    step = 1
    while step < n_row:
        gain_part = gain_part + lax.ppermute(
            gain_part, "row", [(i, i ^ step) for i in range(n_row)])
        step *= 2
    grad_inputs = (
        grad_out.astype(f32) + inv_local * (d_normed - normed * inner[:, None])
    ).astype(bf16)
    return (output, grad_inputs, gain_part, grad_w_gate, grad_w_up, grad_w_down)


def solution(mesh):
    in_specs = (
        P("row", "col"),
        P("col"),
        P("col", "row"),
        P("col", "row"),
        P("row", "col"),
        P("col", "row"),
        P("col", "row"),
        P("row", "col"),
        P("row", "col"),
    )
    out_specs = (
        P("row", "col"),
        P("row", "col"),
        P("col"),
        P("col", "row"),
        P("col", "row"),
        P("row", "col"),
    )
    body = functools.partial(shards, mesh.shape["row"], mesh.shape["col"])

    return jax.shard_map(
        body, mesh=mesh, in_specs=in_specs, out_specs=out_specs, check_vma=False)
```

```python
import functools

import jax
import jax.numpy as jnp
from jax import lax
from jax.experimental import pallas as pl
from jax.experimental.pallas import tpu as pltpu
from jax.sharding import PartitionSpec as P

BLOCK = 64
CORES = 2
epsilon = 1e-05
bf16 = jnp.bfloat16
f32 = jnp.float32


def tile_of(size, limit):
    best = 128
    for tile in range(128, limit + 1, 128):
        if size % tile == 0:
            best = tile
    return best


def lanes(block_mask):
    rows, cols = block_mask.shape
    wide = jnp.broadcast_to(block_mask.astype(f32)[:, :, None], (rows, cols, BLOCK))
    return lax.optimization_barrier(wide.reshape(rows, cols * BLOCK))


def dot(left, right, left_axis, right_axis):
    return lax.dot_general(
        left, right, (((left_axis,), (right_axis,)), ((), ())), preferred_element_type=f32
    )


def keep_rows(mask_ref, row, cols):
    keep = jnp.broadcast_to(mask_ref[pl.ds(row, 1), :], (16, cols))
    return keep.astype(bf16)[None]


def block_rows(value, keep):
    cols = value.shape[1]
    return (value.reshape(BLOCK // 16, 16, cols) * keep).reshape(BLOCK, cols)


def whole(array):
    return pl.BlockSpec(array.shape, lambda *_: (0,) * array.ndim)


def call(body, grid, scalars, operands, in_specs, out_specs, out_shape, scratch,
         flops, moved, aliases=None):
    return pl.pallas_call(
        body,
        grid_spec=pltpu.PrefetchScalarGridSpec(
            num_scalar_prefetch=1,
            grid=grid,
            in_specs=in_specs,
            out_specs=out_specs,
            scratch_shapes=scratch,
        ),
        out_shape=out_shape,
        input_output_aliases=aliases or {},
        compiler_params=pltpu.CompilerParams(vmem_limit_bytes=60 << 20),
        cost_estimate=pl.CostEstimate(
            flops=int(flops), bytes_accessed=int(moved), transcendentals=0),
    )(scalars, *operands)


class Plan:
    def __init__(self, width):
        self.half = width // CORES
        self.tile = tile_of(self.half, 256)
        self.count = self.half // self.tile
        first = (self.count + 1) // 2
        self.chunks = [(0, first)]
        if self.count > first:
            self.chunks.append((first, self.count - first))


def mask_rows(plan, chunk, scalars, w_down, down_lanes):
    first, steps = chunk
    depth, tile = w_down.shape[1], plan.tile

    def body(_, w_ref, k_ref, out_ref):
        start = pl.program_id(0) * plan.count + first + pl.program_id(1)
        for index in range(tile // BLOCK):
            span = pl.ds(index * BLOCK, BLOCK)
            keep = keep_rows(k_ref, start * (tile // BLOCK) + index, depth)
            out_ref[span, :] = block_rows(w_ref[span, :], keep)

    return call(
        body, (CORES, steps), scalars, (w_down, down_lanes),
        [pl.BlockSpec((tile, depth), lambda h, j, s: (h * plan.count + first + j, 0)),
         whole(down_lanes)],
        pl.BlockSpec((tile, depth), lambda h, j, s: (h * steps + j, 0)),
        jax.ShapeDtypeStruct((CORES * steps * tile, depth), bf16), [],
        0, 4 * CORES * depth * steps * tile)


def gathered(shards, scratch):
    @pl.when(pl.program_id(0) == 0)
    def _():
        row = 0
        for ref in shards:
            scratch[row:row + ref.shape[0], :] = ref[...]
            row += ref.shape[0]


def project(side, plan, chunk, halves, tokens, weights, added=None, inverse_gain=None,
            keep=True):
    first, steps = chunk
    local, depth = tokens[0].shape
    rows, tile, count = local * len(tokens), plan.tile, len(tokens)

    def body(_, *refs):
        scratch = refs[-1] if keep else refs[-2]
        g_ref, u_ref, gm_ref, um_ref = refs[count:count + 4]
        rest = refs[count + 4:-1] if keep else refs[count + 4:-2]
        kept_ref = rest[-1] if keep else refs[-1]
        if keep:
            rest = rest[:-1]
        gathered(refs[:count], scratch)
        if inverse_gain is not None:
            gain_ref, out_ref, sum_ref = rest

            @pl.when(pl.program_id(0) == 0)
            def _():
                for row in range(0, rows, local):
                    value = scratch[row:row + local, :].astype(f32) * gain_ref[...]
                    sum_ref[row:row + local, :] = jnp.sum(value * value, axis=1, keepdims=True)
        else:
            out_ref = rest[-1]
        for w_ref, k_ref, lane in ((g_ref, gm_ref, 0), (u_ref, um_ref, tile)):
            for index in range(depth // BLOCK):
                span = pl.ds(index * BLOCK, BLOCK)
                kept_ref[span, lane:lane + tile] = block_rows(
                    w_ref[span, :], keep_rows(k_ref, index, tile))
            value = dot(scratch[...], kept_ref[:, lane:lane + tile], 1, 0)
            if added is not None:
                value += rest[0][:, lane:lane + tile].astype(f32)
            out_ref[:, lane:lane + tile] = value.astype(bf16)

    column = lambda j, h: (0, h[side] * plan.count + first + j)
    weight = pl.BlockSpec((depth, tile), column)
    mask = pl.BlockSpec((depth // BLOCK, tile), column)
    out = pl.BlockSpec((rows, 2 * tile), lambda j, h: (0, j))
    kept = pl.BlockSpec((depth, 2 * tile), lambda j, h: (0, j))
    width = 2 * steps * tile
    extra, extra_specs = [], []
    out_specs = [out]
    shapes = [jax.ShapeDtypeStruct((rows, width), bf16)]
    scratch_shapes = [pltpu.VMEM((rows, depth), bf16)]
    if added is not None:
        extra, extra_specs = [added], [out]
    if inverse_gain is not None:
        extra, extra_specs = [inverse_gain], [whole(inverse_gain)]
        out_specs.append(pl.BlockSpec((rows, 1), lambda j, h: (0, 0)))
        shapes.append(jax.ShapeDtypeStruct((rows, 1), f32))
    if keep:
        out_specs.append(kept)
        shapes.append(jax.ShapeDtypeStruct((depth, width), bf16))
    else:
        scratch_shapes.append(pltpu.VMEM((depth, 2 * tile), bf16))
    return call(
        body, (steps,), halves, (*tokens, *weights, *extra),
        [whole(value) for value in tokens] + [weight, weight, mask, mask] + extra_specs,
        out_specs, shapes, scratch_shapes,
        2 * rows * depth * width, 4 * depth * width + 2 * rows * depth + 4 * rows * width)


def back_project(side, halves, tokens, weight, added=None):
    local, depth = tokens[0].shape
    rows, count = local * len(tokens), len(tokens)
    width = weight.shape[0] // CORES
    tile = tile_of(width, 256)
    steps = width // tile

    def body(_, *refs):
        scratch, out_ref, w_ref = refs[-1], refs[-2], refs[count]
        gathered(refs[:count], scratch)
        value = dot(scratch[...], w_ref[...], 1, 1)
        if added is not None:
            value += refs[count + 1][...].astype(f32)
        out_ref[...] = value.astype(bf16)

    out = pl.BlockSpec((rows, tile), lambda i, h: (0, i))
    extra = () if added is None else (added,)
    return call(
        body, (steps,), halves, (*tokens, weight, *extra),
        [whole(value) for value in tokens]
        + [pl.BlockSpec((tile, depth), lambda i, h: (h[side] * steps + i, 0))]
        + [out] * len(extra),
        out, jax.ShapeDtypeStruct((rows, width), bf16), [pltpu.VMEM((rows, depth), bf16)],
        2 * rows * depth * width, 2 * depth * width + 2 * rows * depth + 2 * rows * width)


def activate(plan, scalars, scale, pair, grads, with_hidden):
    rows, width = scale.shape[0], pair[0][0].shape[1]
    tile = plan.tile
    flat = [array for piece in pair for array in piece]
    count = len(flat)
    operands = [scale, *flat, *(grads or ())]
    in_specs = [whole(scale)]
    in_specs += [pl.BlockSpec((a.shape[0], 2 * tile), lambda j, s: (0, j)) for a in flat]
    step = 96 if all(a.shape[0] % 96 == 0 for a in flat) else 16
    in_specs += [pl.BlockSpec((rows, tile), lambda j, s: (0, j)) for _ in grads or ()]
    out_specs, shapes = [], []
    if grads:
        out_specs.append(pl.BlockSpec((rows, 2 * tile), lambda j, s: (0, j)))
        shapes.append(jax.ShapeDtypeStruct((rows, width), bf16))
    if with_hidden:
        out_specs.append(pl.BlockSpec((rows, tile), lambda j, s: (0, j)))
        shapes.append(jax.ShapeDtypeStruct((rows, width // 2), bf16))

    def summed(refs, low, high, lane):
        total = None
        for ref in refs:
            term = ref[low:high, lane:lane + tile].astype(f32)
            total = term if total is None else total + term
        return total

    def body(_, s_ref, *refs):
        outs = refs[len(operands) - 1:]
        for low in range(0, rows, step):
            high = low + step
            factor = s_ref[low:high, :]
            base, first = 0, 0
            for piece in pair:
                if low < base + piece[0].shape[0]:
                    break
                base, first = base + piece[0].shape[0], first + len(piece)
            source = refs[first:first + len(piece)]
            gate = summed(source, low - base, high - base, 0) * factor
            up = summed(source, low - base, high - base, tile) * factor
            sigma = jax.nn.sigmoid(gate)
            silu = gate * sigma
            if grads:
                grad = summed(refs[count:len(operands) - 1], low, high, 0)
                d_gate = grad * up * sigma * (1.0 + gate * (1.0 - sigma))
                outs[0][low:high, :tile] = d_gate.astype(bf16)
                outs[0][low:high, tile:] = (grad * silu).astype(bf16)
            if with_hidden:
                outs[-1][low:high, :] = (silu * up).astype(bf16)

    return call(
        body, (width // 2 // tile,), scalars, operands, in_specs,
        out_specs, shapes, [], 0, 2 * sum(a.size for a in operands) + 3 * rows * width)


def down_product(halves, hidden, weights):
    rows, depth = hidden[0][0].shape[0], weights[0].shape[1]
    tile = tile_of(depth, 256)
    operands, in_specs = [], []
    for pair, weight in zip(hidden, weights):
        width = weight.shape[0] // CORES
        for side, value in enumerate(pair):
            operands += [value, weight]
            in_specs += [whole(value), pl.BlockSpec(
                (width, tile), lambda i, h, side=side: (h[side], i))]

    def body(_, *refs):
        value = None
        for h_ref, w_ref in zip(refs[:-1:2], refs[1:-1:2]):
            term = dot(h_ref[...], w_ref[...], 1, 0)
            value = term if value is None else value + term
        refs[-1][...] = value.astype(bf16)

    total = sum(weight.size for weight in weights)
    return call(
        body, (depth // tile,), halves, operands, in_specs,
        pl.BlockSpec((rows, tile), lambda i, h: (0, i)),
        jax.ShapeDtypeStruct((rows, depth), bf16), [],
        2 * rows * total, 2 * total + 2 * rows * (total // depth + depth))


def input_cotangent(scalars, pair, weights, added, dtype):
    rows = pair[0].shape[0]
    depth, width = weights[0].shape
    tile = tile_of(depth, 256)
    side = pl.BlockSpec((tile, width), lambda i, h: (i, 0))
    extra = () if added is None else (added,)

    def body(_, m_ref, o_ref, wm_ref, wo_ref, *rest):
        value = dot(m_ref[...], wm_ref[...], 1, 1) + dot(o_ref[...], wo_ref[...], 1, 1)
        if added is not None:
            value += rest[0][...]
        rest[-1][...] = value.astype(dtype)

    return call(
        body, (depth // tile,), scalars, (*pair, *weights, *extra),
        [whole(pair[0]), whole(pair[1]), side, side]
        + [pl.BlockSpec((a.shape[0], tile), lambda i, h: (0, i)) for a in extra],
        pl.BlockSpec((rows, tile), lambda i, h: (0, i)),
        jax.ShapeDtypeStruct((rows, depth), dtype), [],
        4 * rows * depth * width, 4 * depth * width + 4 * rows * width + 4 * rows * depth)


def turn(scalars, scale, pieces):
    rows, depth = scale.shape[0], pieces[0].shape[1]
    tile = tile_of(depth, 256)

    def body(_, s_ref, *refs):
        out_ref, scratch = refs[-2:]
        first = 0
        for ref in refs[:-2]:
            span = slice(first, first + ref.shape[0])
            scratch[span, :] = (ref[...].astype(f32) * s_ref[span, :]).astype(bf16)
            first += ref.shape[0]
        out_ref[...] = scratch[...].T

    return call(
        body, (depth // tile,), scalars, (scale, *pieces),
        [whole(scale)] + [pl.BlockSpec((p.shape[0], tile), lambda i, s: (0, i)) for p in pieces],
        pl.BlockSpec((tile, rows), lambda i, s: (i, 0)),
        jax.ShapeDtypeStruct((depth, rows), bf16), [pltpu.VMEM((rows, tile), bf16)],
        0, 4 * rows * depth)


def gate_up_grads(plan, chunk, halves, turned, mine, other, gate_lanes, up_lanes, earlier,
                  single=None):
    first, steps = chunk
    skipped = 0
    if single is not None:
        first, steps, skipped = first + single, 1, single
    depth, rows = turned.shape
    tile = plan.tile
    n_mine = len(mine)

    def body(_, x_ref, *refs):
        sides = refs[:n_mine], refs[n_mine:2 * n_mine]
        masks = refs[2 * n_mine:2 * n_mine + 2]
        outs, scratch = refs[-3:-1], refs[-1]

        def collect(pieces):
            row = 0
            for ref in pieces:
                scratch[row:row + ref.shape[0], :] = ref[...]
                row += ref.shape[0]

        pl.when(pl.program_id(0) == 0)(lambda: collect(sides[0]))
        pl.when(pl.program_id(0) == 1)(lambda: collect(sides[1]))
        for index in range(2):
            right = scratch[:, index * tile:(index + 1) * tile]
            value = dot(x_ref[...], right, 1, 0).astype(bf16)
            for block in range(depth // BLOCK):
                span = slice(block * BLOCK, (block + 1) * BLOCK)
                outs[index][span, :] = block_rows(
                    value[span, :], keep_rows(masks[index], block, tile))

    column = lambda p, j, h: (0, h[p] * plan.count + first + j)
    in_specs = [whole(turned)]
    in_specs += [pl.BlockSpec((a.shape[0], 2 * tile), lambda p, j, h: (
        0, skipped + jnp.where(p == 0, j, steps - 1))) for a in mine]
    in_specs += [pl.BlockSpec((a.shape[0], 2 * tile), lambda p, j, h: (
        0, skipped + jnp.where(p == 0, 0, j))) for a in other]
    in_specs += [pl.BlockSpec((depth // BLOCK, tile), column)] * 2
    out = pl.BlockSpec((depth, tile), column)
    shape = jax.ShapeDtypeStruct((depth, plan.half * CORES), bf16)
    operands = [turned, *mine, *other, gate_lanes, up_lanes]
    aliases = None
    if earlier is not None:
        aliases = {len(operands) + 1: 0, len(operands) + 2: 1}
        operands += earlier
        in_specs += [pl.BlockSpec(memory_space=pl.ANY)] * 2
    return call(
        body, (CORES, steps), halves, operands, in_specs, [out, out], [shape, shape],
        [pltpu.VMEM((rows, 2 * tile), bf16)],
        8 * rows * depth * steps * tile,
        2 * rows * depth + 8 * rows * steps * tile + 8 * depth * steps * tile, aliases)


def down_grads(plan, halves, hidden, grads, down_lanes):
    rows, depth = hidden[0][0].shape[0], grads[0].shape[1]
    tile = tile_of(depth, 256)
    operands, places = [], []
    for pair, (first, steps) in zip(hidden, plan.chunks):
        for side, value in enumerate(pair):
            operands.append(value)
            places.append((side, first * plan.tile))
    count = len(operands)
    width = plan.half * CORES

    def body(half_ref, *refs):
        turned, right, out_ref = refs[-2], refs[-1], refs[-3]

        @pl.when(pl.program_id(0) == 0)
        def _():
            for ref, (side, first) in zip(refs[:count], places):
                start = pl.multiple_of(half_ref[side] * plan.half + first, 128)
                for lane in range(0, ref.shape[1], plan.tile):
                    turned[pl.ds(start + lane, plan.tile), :] = ref[:, lane:lane + plan.tile].T

        row = 0
        for ref in refs[count:count + len(grads)]:
            right[row:row + ref.shape[0], :] = ref[...]
            row += ref.shape[0]
        k_ref = refs[count + len(grads)]
        piece = plan.tile
        for part in range(width // piece):
            value = dot(turned[part * piece:(part + 1) * piece, :], right[...], 1, 0).astype(bf16)
            for block in range(piece // BLOCK):
                low = part * piece + block * BLOCK
                out_ref[low:low + BLOCK, :] = block_rows(
                    value[block * BLOCK:(block + 1) * BLOCK, :],
                    keep_rows(k_ref, low // BLOCK, tile))

    column = lambda i, h: (0, i)
    return call(
        body, (depth // tile,), halves, (*operands, *grads, down_lanes),
        [whole(value) for value in operands]
        + [pl.BlockSpec((g.shape[0], tile), column) for g in grads]
        + [pl.BlockSpec((down_lanes.shape[0], tile), column)],
        pl.BlockSpec((width, tile), column),
        jax.ShapeDtypeStruct((width, depth), bf16),
        [pltpu.VMEM((width, rows), bf16), pltpu.VMEM((rows, tile), bf16)],
        2 * rows * depth * width, 2 * depth * width + 2 * rows * width + 2 * rows * depth)


def after(value, *others):
    return lax.optimization_barrier((value, *others))[0]


def shards(n_row, n_col, inputs, norm_gain, w_gate, w_up, w_down,
           mask_gate, mask_up, mask_down, grad_out):
    n_chip = n_col // CORES
    local, width = inputs.shape
    features = width * n_col
    plan = Plan(w_gate.shape[1])
    chunks = plan.chunks
    cycle = list(range(0, n_row, 2)) + list(range(n_row - 1, 0, -2))
    ahead = [(cycle[i], cycle[(i + 1) % n_row]) for i in range(n_row)]
    behind = [(b, a) for a, b in ahead]
    swap = [(i, i ^ 1) for i in range(n_col)]
    n_ahead, n_behind = n_row // 2, (n_row - 1) // 2

    def to_partner(value):
        return lax.ppermute(value, "col", swap)

    def from_chips(value):
        return [
            lax.ppermute(value, "col", [(i, (i + CORES * k) % n_col) for i in range(n_col)])
            for k in range(1, n_chip)
        ]

    def total_over_chips(value):
        total = value
        for other in from_chips(value):
            total = total + other
        return total

    offsets = [0]
    for k in range(1, n_ahead + 1):
        offsets.append(-k)
        if k <= n_behind:
            offsets.append(k)

    core = lax.rem(lax.axis_index("col"), CORES).astype(jnp.int32)
    halves = jnp.stack([core, 1 - core])

    inputs_wide = inputs.astype(f32)
    scaled = (inputs_wide * norm_gain).astype(bf16)

    def ring_step(found, k, *ready):
        found[-k] = lax.ppermute(after(found[1 - k], *ready), "row", ahead)
        if k <= n_behind:
            found[k] = lax.ppermute(after(found[k - 1], *ready), "row", behind)

    shard = {0: scaled}
    ring_step(shard, 1)
    gate_lanes, up_lanes = lanes(mask_gate), lanes(mask_up)
    weights = (w_gate, w_up, gate_lanes, up_lanes)
    inverse_gain = (1.0 / norm_gain)[None]
    ring_step(shard, 2, gate_lanes, up_lanes)
    near = [shard[offset] for offset in offsets[:3]]
    sent0n, squares_near = project(
        1, plan, chunks[0], halves, near, weights,
        inverse_gain=inverse_gain, keep=False)
    ring_step(shard, 3, sent0n)
    got0n = to_partner(sent0n)
    down_lanes = lanes(after(mask_down, sent0n))
    own0n, = project(
        0, plan, chunks[0], after(halves, sent0n), near, weights, got0n, keep=False)
    others0n = from_chips(own0n)
    for k in range(4, n_ahead + 1):
        ring_step(shard, k, own0n)
    dn = [mask_rows(plan, chunks[0], after(halves, own0n), w_down, down_lanes)]
    far = [shard[offset] for offset in offsets[3:]]
    tokens = near + far
    grad_shard = {0: after(grad_out, *far)}
    ring_step(grad_shard, 1)
    sent0f, squares_far, kept0_o = project(
        1, plan, chunks[0], after(halves, dn[0]), far, weights,
        inverse_gain=inverse_gain)
    ring_step(grad_shard, 2, sent0f)
    got0f = to_partner(sent0f)
    own0f, kept0_m = project(
        0, plan, chunks[0], after(halves, sent0f), far, weights, got0f)
    others0f = from_chips(after(own0f, *others0n))
    squares = jnp.concatenate([squares_near[:, 0], squares_far[:, 0]])
    squares = squares + to_partner(squares)
    for other in from_chips(squares):
        squares = squares + other
    ring_step(grad_shard, 3, own0f)
    sent1, kept1_o = project(1, plan, chunks[1], after(halves, own0f), tokens, weights)
    scale = lax.rsqrt(after(squares, sent1) / features + epsilon)[:, None]
    for k in range(4, n_ahead + 1):
        ring_step(grad_shard, k, sent1)
    turned = turn(after(halves, sent1), scale, tokens)
    grads = [grad_shard[offset] for offset in offsets]
    sent_b0 = back_project(1, after(halves, turned), grads, dn[0])
    own_b0 = back_project(0, halves, grads, dn[0], to_partner(sent_b0))
    others_b0 = from_chips(after(own_b0, *others0f))
    own1, kept1_m = project(
        0, plan, chunks[1], after(halves, own_b0), tokens, weights, to_partner(sent1))
    others1 = from_chips(after(own1, *others_b0))
    dn.append(mask_rows(plan, chunks[1], after(halves, own1), w_down, down_lanes))
    sent_b1 = back_project(1, halves, grads, dn[1])
    own_b1 = back_project(0, halves, grads, dn[1], to_partner(sent_b1))
    cot0, hidden0 = activate(plan, after(halves, own_b1), scale,
                             [[own0n, *others0n], [own0f, *others0f]],
                             [own_b0, *others_b0], True)
    cot0 = (cot0, to_partner(cot0))
    hidden0 = (hidden0, to_partner(hidden0))
    partial = input_cotangent(halves, cot0, (kept0_m, kept0_o), None, f32)
    grad_gu = gate_up_grads(plan, chunks[0], after(halves, partial), turned,
                            cot0[:1], cot0[1:], gate_lanes, up_lanes, None)

    others_b1 = from_chips(after(own_b1, *others1))
    hidden1, = activate(plan, after(halves, grad_gu[0]), scale, [[own1, *others1]],
                        None, True)
    hidden1 = (hidden1, to_partner(hidden1))
    mixed = down_product(halves, (hidden0, hidden1), dn)

    def scatter(parts):
        back = parts(-n_ahead)
        front = parts(n_behind)
        for k in range(1, n_ahead + 1):
            back = lax.ppermute(back, "row", behind)
            if k < n_ahead:
                back = (back.astype(f32) + parts(k - n_ahead).astype(f32)).astype(bf16)
            if k <= n_behind:
                front = lax.ppermute(front, "row", ahead)
                if k < n_behind:
                    front = (front.astype(f32) + parts(n_behind - k).astype(f32)).astype(bf16)
        return back.astype(f32) + front.astype(f32) + parts(0).astype(f32)

    def part_of(value):
        parts = {offset: lax.slice_in_dim(value, i * local, (i + 1) * local, axis=0)
                 for i, offset in enumerate(offsets)}
        return lambda offset: parts[offset]

    output = (inputs_wide + scatter(part_of(mixed))).astype(bf16)
    cot1, = activate(plan, after(halves, mixed), scale, [[own1, *others1]],
                     [own_b1, *others_b1], False)
    cot1 = (cot1, to_partner(cot1))
    norm_all = input_cotangent(halves, cot1, (kept1_m, kept1_o), partial, bf16)
    d_norm_in = scatter(part_of(norm_all))
    grad_w_down = down_grads(plan, after(halves, norm_all), (hidden0, hidden1),
                             grads, down_lanes)
    ready = grad_w_down
    for index in range(chunks[1][1]):
        grad_gu = gate_up_grads(
            plan, chunks[1], after(halves, ready), turned,
            cot1[:1], cot1[1:], gate_lanes, up_lanes, grad_gu, index)
        ready = grad_gu[0]
    grad_w_gate, grad_w_up = grad_gu

    inv_local = scale[:local]
    normed = inputs_wide * inv_local
    d_normed = d_norm_in * norm_gain
    inner = jnp.sum(d_normed * normed, axis=1)
    inner = inner + to_partner(inner)
    inner = total_over_chips(inner) / features
    gain_part = jnp.sum(d_norm_in * normed, axis=0)
    step = 1
    while step < n_row:
        gain_part = gain_part + lax.ppermute(
            gain_part, "row", [(i, i ^ step) for i in range(n_row)])
        step *= 2
    grad_inputs = (
        grad_out.astype(f32) + inv_local * (d_normed - normed * inner[:, None])
    ).astype(bf16)
    return (output, grad_inputs, gain_part, grad_w_gate, grad_w_up, grad_w_down)


def solution(mesh):
    in_specs = (
        P("row", "col"),
        P("col"),
        P("col", "row"),
        P("col", "row"),
        P("row", "col"),
        P("col", "row"),
        P("col", "row"),
        P("row", "col"),
        P("row", "col"),
    )
    out_specs = (
        P("row", "col"),
        P("row", "col"),
        P("col"),
        P("col", "row"),
        P("col", "row"),
        P("row", "col"),
    )
    body = functools.partial(shards, mesh.shape["row"], mesh.shape["col"])

    return jax.shard_map(
        body, mesh=mesh, in_specs=in_specs, out_specs=out_specs, check_vma=False)
```
